512 devices in a mesh: ctx: 16 (over z_lo, core), head: 32 (over x, y, z_hi).
Axes of the slice: x: 4, y: 4, z: 16 (z_hi: 2, z_lo: 8; z = z_hi * 8 + z_lo), core: 2. Of those that a mesh axis runs over, the one named last changes fastest.
Arguments:
- queries: bfloat16 [256, 24576], P('ctx', 'head'), may hold values from -8 to 8
- cache: bfloat16 [32768, 576], P(('ctx', 'head')), may hold values from -8 to 8
- key_up_weight: bfloat16 [128, 128, 512], P('head', None, 'ctx'), may hold values from -0.5 to 0.5
- value_up_weight: bfloat16 [128, 128, 512], P('head', None, 'ctx'), may hold values from -1.5 to 1.5
- prior_len: int32 [1], replicated, may hold values from 0 to 32512
Outputs:
- attended: bfloat16 [256, 16384], P('ctx', 'head')
The draws below stay inside these ranges and needn't reach their ends.
All inputs are finite; a program needn't handle non-finite values.
Results may differ from the reference program's by a relative error of at most 0.02.
Values may be sent and summed in bfloat16 or wider, within the bound.
No kernel may reach another device: no remote copies, remote signals or barrier semaphores. Data moves between devices by JAX's collectives and lax.ppermute only.
A program may use at most 128 MiB of HBM per device.

```python
import jax
import jax.numpy as jnp
from jax import lax

HEAD_TOTAL = 128
PLAIN_WIDTH = 128
ROTARY_WIDTH = 64
LATENT_WIDTH = 512
VALUE_WIDTH = 128
QTOK = 256
CACHE = 32768


def draw_cache(key, part):
    latent_row_width = LATENT_WIDTH + ROTARY_WIDTH
    sampled_inputs = jnp.clip(jax.random.normal(jax.random.fold_in(key, 1), (CACHE, latent_row_width), jnp.float32), -6.0, 6.0)
    return sampled_inputs.astype(jnp.bfloat16)


def draw_queries(key, part):
    sampled_inputs = jnp.clip(jax.random.normal(jax.random.fold_in(key, 21), (QTOK, HEAD_TOTAL, PLAIN_WIDTH + ROTARY_WIDTH), jnp.float32), -6.0, 6.0)
    return sampled_inputs.reshape(QTOK, HEAD_TOTAL * (PLAIN_WIDTH + ROTARY_WIDTH)).astype(jnp.bfloat16)


def level_of(key, extent, shards, smallest, largest):
    factor_of = 1.0
    for axis_at, blocks in shards:
        draws = jax.random.uniform(jax.random.fold_in(jax.random.fold_in(key, 6), axis_at), (blocks,), jnp.float32, smallest / len(shards), largest / len(shards))
        factor_of = factor_of * jnp.repeat(jnp.exp(draws), extent[axis_at] // blocks).reshape((-1,) + (1,) * (len(extent) - 1 - axis_at))
    return factor_of


def centred(own_key, shape, width, bound, pieces=(), kind=jnp.bfloat16):
    entries = width * jax.random.normal(own_key, shape, jnp.float32)
    if pieces:
        entries = entries * level_of(own_key, shape, pieces, -0.22, 0.18)
    return jnp.clip(entries, -bound, bound).astype(kind)


def setup_inputs(seed: int = 0) -> dict:
    arg_keys = jax.random.split(jax.random.key(seed), 6)
    return {
        "queries": draw_queries(jax.random.fold_in(arg_keys[5], 71), 0),
        "cache": draw_cache(jax.random.fold_in(arg_keys[5], 71), 0),
        "key_up_weight": centred(arg_keys[2], (HEAD_TOTAL, PLAIN_WIDTH, LATENT_WIDTH), PLAIN_WIDTH ** -0.5, 0.5, ((0, 32), (2, 16))),
        "value_up_weight": centred(arg_keys[3], (HEAD_TOTAL, VALUE_WIDTH, LATENT_WIDTH), 0.25, 1.5, ((0, 32), (2, 16))),
        "prior_len": jax.random.randint(arg_keys[4], (1,), 0, CACHE - QTOK + 1).astype(jnp.int32),
    }


def reference(queries, cache, key_up_weight, value_up_weight, prior_len):
    split_rows = queries.reshape(QTOK, HEAD_TOTAL, PLAIN_WIDTH + ROTARY_WIDTH)
    query_place = prior_len[0] + jnp.arange(QTOK, dtype=jnp.int32)
    key_place = jnp.arange(CACHE, dtype=jnp.int32)
    visible = key_place[None, :] <= query_place[:, None]
    key_matrix = cache.astype(jnp.float32)
    value_matrix = key_matrix[:, :LATENT_WIDTH]
    score_scale = (PLAIN_WIDTH + ROTARY_WIDTH) ** -0.5

    def one_head(inputs):
        head_rows, key_panel, value_panel = inputs
        latent = jnp.dot(head_rows[:, :PLAIN_WIDTH], key_panel, preferred_element_type=jnp.float32).astype(jnp.bfloat16)
        joined = jnp.concatenate([latent, head_rows[:, PLAIN_WIDTH:]], axis=1).astype(jnp.float32)
        scores = jnp.dot(joined, key_matrix.T, precision=lax.Precision.HIGHEST) * score_scale
        scores = jnp.where(visible, scores, jnp.float32(-1e30))
        row_peak = jnp.max(scores, axis=1)
        probabilities = jnp.where(visible, jnp.exp(scores - row_peak[:, None]), jnp.float32(0.0))
        row_total = jnp.sum(probabilities, axis=1)
        rounded = probabilities.astype(jnp.bfloat16).astype(jnp.float32)
        latent_out = jnp.dot(rounded, value_matrix, precision=lax.Precision.HIGHEST)
        projected = jnp.dot(latent_out, value_panel.astype(jnp.float32).T, precision=lax.Precision.HIGHEST)
        return (projected / row_total[:, None]).astype(jnp.bfloat16)

    per_head = lax.map(one_head, (jnp.transpose(split_rows, (1, 0, 2)), key_up_weight, value_up_weight))
    return jnp.transpose(per_head, (1, 0, 2)).reshape(QTOK, HEAD_TOTAL * VALUE_WIDTH)
```

```python
import math

import jax
import jax.numpy as jnp
from jax import lax
from jax.experimental import pallas as pl
from jax.experimental.pallas import tpu as pltpu
from jax.sharding import Mesh
from jax.sharding import PartitionSpec as P

PLAIN = 128
ROT = 64
LATENT = 512
VALUE = 128
HEADS = 4
WIDTH = LATENT + ROT
TOK = 16
NEG = -1e30
LOG2_SCALE = (PLAIN + ROT) ** (-0.5) * math.log2(math.e)
VMEM_LIMIT = 48 * 1024 * 1024

f32 = jnp.float32
bf16 = jnp.bfloat16


def vmem():
    return pl.BlockSpec(memory_space=pltpu.VMEM)


def smem():
    return pl.BlockSpec(memory_space=pltpu.SMEM)


def chain_slot(zl, co, my_zl, my_co):
    dz = lax.bitwise_xor(my_zl, zl)
    dc = lax.bitwise_xor(my_co, co)
    a = lax.shift_right_logical(dz, 2)
    b = lax.bitwise_and(lax.shift_right_logical(dz, 1), 1)
    c = lax.bitwise_and(dz, 1)
    return dc * 8 + c * 4 + b * 2 + a


def query_kernel(place, pack, q_out, wv_out, pieces, panel):
    my_zl, my_co = place[0], place[1]
    for co in range(2):
        for zl in range(8):
            slot = chain_slot(jnp.int32(zl), jnp.int32(co), my_zl, my_co)
            rows = pl.ds((co * 8 + zl) * TOK, TOK)
            cols = pl.ds((zl * 2 + co) * 32, 32)
            for k in range(6):
                pieces[k, rows, :] = pack[slot, pl.ds(k * TOK, TOK), :]
            for h in range(HEADS):
                panel[h, cols, :] = pack[slot, pl.ds(96 + h * 32, 32), :]
                wv_out[h, cols, :] = pack[slot, pl.ds(224 + h * 32, 32), :]
    for h in range(HEADS):
        k = (h // 2) * 3
        if h % 2 == 0:
            plain = pieces[k]
            rot = pieces[k + 1][:, :ROT]
        else:
            plain = jnp.concatenate([pieces[k + 1][:, ROT:], pieces[k + 2][:, :ROT]], axis=1)
            rot = pieces[k + 2][:, ROT:]
        lat = lax.dot_general(
            plain, panel[h], (((1,), (1,)), ((), ())), preferred_element_type=f32
        )
        q_out[h, :, :LATENT] = lat.astype(bf16)
        q_out[h, :, LATENT:] = rot


def split3(x):
    hi = x.astype(bf16)
    r = x - hi.astype(f32)
    mid = r.astype(bf16)
    lo = (r - mid.astype(f32)).astype(bf16)
    return hi, mid, lo


def pack_lse(columns, shape):
    lane = lax.broadcasted_iota(jnp.int32, shape, len(shape) - 1)
    tile = jnp.zeros(shape, f32)
    for h, column in enumerate(columns):
        for p, part in enumerate(split3(column)):
            tile = jnp.where(lane == 3 * h + p, part.astype(f32), tile)
    return tile.astype(bf16)


def attention_kernel(prior, kpos, q, c0, c1, c2, c3, wv, out):
    row = lax.broadcasted_iota(jnp.int32, (256, 1), 0)
    zl = lax.bitwise_and(lax.shift_right_logical(row, 4), 7)
    co = lax.shift_right_logical(row, 7)
    token = zl * 32 + co * 16 + lax.bitwise_and(row, 15)
    limit = prior[0] + token
    chunks = (c0, c1, c2, c3)
    lses = []
    for h in range(HEADS):
        scores = []
        for j, c in enumerate(chunks):
            s = lax.dot_general(
                q[h], c[...], (((1,), (1,)), ((), ())), preferred_element_type=f32
            )
            seen = kpos[:, pl.ds(j * 512, 512)] <= limit
            scores.append(jnp.where(seen, s * LOG2_SCALE, NEG))
        peak = scores[0].max(axis=1, keepdims=True)
        for s in scores[1:]:
            peak = jnp.maximum(peak, s.max(axis=1, keepdims=True))
        total = jnp.zeros((256, 1), f32)
        acc = jnp.zeros((256, LATENT), f32)
        for s, c in zip(scores, chunks):
            p = jnp.exp2(s - peak)
            total = total + p.sum(axis=1, keepdims=True)
            acc = acc + jnp.dot(p.astype(bf16), c[:, :LATENT], preferred_element_type=f32)
        latent = (acc / total).astype(bf16)
        o = jnp.dot(latent, wv[h], preferred_element_type=f32).astype(bf16)
        for g in range(16):
            out[g // 8, g % 8, h] = o[g * TOK : (g + 1) * TOK]
        lses.append(peak + jnp.log2(total))
    tile = pack_lse(lses, (256, 128))
    for g in range(16):
        out[g // 8, g % 8, HEADS] = tile[g * TOK : (g + 1) * TOK]


def lse_column(tile, h):
    t = tile.astype(f32)
    k = 3 * h
    return t[:, k : k + 1] + t[:, k + 1 : k + 2] + t[:, k + 2 : k + 3]


def pair_kernel(a, b, out):
    for g in range(8):
        ta, tb = a[g, HEADS], b[g, HEADS]
        lses = []
        for h in range(HEADS):
            la, lb = lse_column(ta, h), lse_column(tb, h)
            top = jnp.maximum(la, lb)
            wa, wb = jnp.exp2(la - top), jnp.exp2(lb - top)
            total = wa + wb
            o = (a[g, h].astype(f32) * wa + b[g, h].astype(f32) * wb) / total
            out[g, h] = o.astype(bf16)
            lses.append(top + jnp.log2(total))
        out[g, HEADS] = pack_lse(lses, (TOK, 128))


def final_kernel(x, out):
    for h in range(HEADS):
        lses = [lse_column(x[g, HEADS], h) for g in range(8)]
        top = lses[0]
        for l in lses[1:]:
            top = jnp.maximum(top, l)
        acc = jnp.zeros((TOK, VALUE), f32)
        total = jnp.zeros((TOK, 1), f32)
        for g in range(8):
            w = jnp.exp2(lses[g] - top)
            total = total + w
            acc = acc + x[g, h].astype(f32) * w
        out[:, h * VALUE : (h + 1) * VALUE] = (acc / total).astype(bf16)


def swap(x, axis, n, d):
    return lax.ppermute(x, axis, [(i, i ^ d) for i in range(n)])


def call(kernel, shape, n_in, name, scratch=(), scalars=0):
    return pl.pallas_call(
        kernel,
        out_shape=shape,
        in_specs=[smem()] * scalars + [vmem()] * n_in,
        out_specs=jax.tree.map(lambda _: vmem(), shape),
        scratch_shapes=list(scratch),
        compiler_params=pltpu.CompilerParams(vmem_limit_bytes=VMEM_LIMIT),
        name=name,
    )


def per_device(queries, cache, key_up_weight, value_up_weight, prior_len):
    zl, co = lax.axis_index("zl"), lax.axis_index("co")
    x, y, zh = lax.axis_index("x"), lax.axis_index("y"), lax.axis_index("zh")

    pack = jnp.concatenate(
        [
            queries.reshape(TOK, 6, 128).transpose(1, 0, 2).reshape(96, 128),
            key_up_weight.transpose(0, 2, 1).reshape(128, 128),
            value_up_weight.transpose(0, 2, 1).reshape(128, 128),
        ],
        axis=0,
    )[None]
    mirror = lax.ppermute(cache, ("zl", "zh"), [(i, 15 - i) for i in range(16)])
    for d in (4, 2, 1):
        pack = jnp.concatenate([pack, swap(pack, "zl", 8, d)], axis=0)
    pack = jnp.concatenate([pack, swap(pack, "co", 2, 1)], axis=0)
    pair = jnp.concatenate([cache, mirror], axis=0)
    quad = jnp.concatenate([pair] + [swap(pair, "x", 4, d) for d in (1, 2, 3)], axis=0)
    chunks = [quad] + [swap(quad, "y", 4, d) for d in (1, 2, 3)]

    place = jnp.stack([zl, co]).astype(jnp.int32)
    q, wv = call(
        query_kernel,
        (
            jax.ShapeDtypeStruct((HEADS, 256, WIDTH), bf16),
            jax.ShapeDtypeStruct((HEADS, LATENT, VALUE), bf16),
        ),
        1,
        "query",
        (pltpu.VMEM((6, 256, 128), bf16), pltpu.VMEM((HEADS, LATENT, 128), bf16)),
        1,
    )(place, pack)

    n = jnp.arange(2048, dtype=jnp.int32)
    dy, dx, m, i = n >> 9, (n >> 7) & 3, (n >> 6) & 1, n & 63
    src_z, src_h = jnp.where(m == 1, 7 - zl, zl), jnp.where(m == 1, 1 - zh, zh)
    head = ((x ^ dx) * 4 + (y ^ dy)) * 2 + src_h
    kpos = (((src_z * 2 + co) * 32 + head) * 64 + i).astype(jnp.int32)[None]

    part = call(
        attention_kernel,
        jax.ShapeDtypeStruct((2, 8, HEADS + 1, TOK, 128), bf16),
        7,
        "attention",
        (),
        1,
    )(prior_len, kpos, q, *chunks, wv)

    mine = lax.dynamic_index_in_dim(part, co, 0, keepdims=False)
    other = lax.dynamic_index_in_dim(part, 1 - co, 0, keepdims=False)
    got = swap(other, "co", 2, 1)
    merged = call(
        pair_kernel, jax.ShapeDtypeStruct((8, HEADS + 1, TOK, 128), bf16), 2, "pair"
    )(mine, got)
    spread = lax.all_to_all(merged, "zl", 0, 0, tiled=True)
    return call(
        final_kernel, jax.ShapeDtypeStruct((TOK, HEADS * VALUE), bf16), 1, "final"
    )(spread)


def solution(mesh):
    fine = Mesh(mesh.devices.reshape(8, 2, 4, 4, 2), ("zl", "co", "x", "y", "zh"))
    ctx, head = ("zl", "co"), ("x", "y", "zh")
    return jax.shard_map(
        per_device,
        mesh=fine,
        in_specs=(P(ctx, head), P(ctx + head, None), P(head, None, ctx), P(head, None, ctx), P()),
        out_specs=P(ctx, head),
        check_vma=False,
    )
```

```python
import math

import jax
import jax.numpy as jnp
from jax import lax
from jax.experimental import pallas as pl
from jax.experimental.pallas import tpu as pltpu
from jax.sharding import Mesh
from jax.sharding import PartitionSpec as P

PLAIN = 128
ROT = 64
LATENT = 512
VALUE = 128
HEADS = 4
WIDE = LATENT + 2 * ROT
TOK = 16
ROWS = 256
NEG = -1e30
LOG2_SCALE = (PLAIN + ROT) ** (-0.5) * math.log2(math.e)
VMEM_LIMIT = 40 * 1024 * 1024

CTX = ("zl", "co")
f32 = jnp.float32
bf16 = jnp.bfloat16


def vmem():
    return pl.BlockSpec(memory_space=pltpu.VMEM)


def call(kernel, shape, n_in, name, scratch=()):
    return pl.pallas_call(
        kernel,
        out_shape=shape,
        in_specs=[pl.BlockSpec(memory_space=pltpu.SMEM)] + [vmem()] * n_in,
        out_specs=jax.tree.map(lambda _: vmem(), shape),
        scratch_shapes=list(scratch),
        compiler_params=pltpu.CompilerParams(vmem_limit_bytes=VMEM_LIMIT),
        cost_estimate=pl.CostEstimate(flops=1, transcendentals=0, bytes_accessed=1),
        name=name,
    )


def shaped(shape, dtype=bf16):
    return jax.ShapeDtypeStruct(shape, dtype)


def prepare_kernel(queries_hbm, cache_hbm, wk_hbm, wv_hbm, shard, pack, queries, cache, sems):
    copies = [
        pltpu.make_async_copy(src, dst, sems.at[i])
        for i, (src, dst) in enumerate(
            (
                (cache_hbm, cache),
                (queries_hbm, queries),
                (wk_hbm, pack.at[0, 96:224, :]),
                (wv_hbm, pack.at[0, 224:352, :]),
            )
        )
    ]
    for c in copies:
        c.start()
    copies[0].wait()
    shard[0, :64, :] = cache[:, :LATENT]
    rot = cache[:, LATENT:]
    pairs = jnp.concatenate([rot[:32], rot[32:]], axis=1)
    for k in range(4):
        shard[0, 64:72, 128 * k : 128 * (k + 1)] = pairs[8 * k : 8 * (k + 1)]
    copies[1].wait()
    for k in range(6):
        pack[0, TOK * k : TOK * (k + 1), :] = queries[:, 128 * k : 128 * (k + 1)]
    copies[2].wait()
    copies[3].wait()


def prepare(queries, cache, wk, wv):
    return pl.pallas_call(
        prepare_kernel,
        out_shape=(shaped((1, 72, LATENT)), shaped((1, 352, 128))),
        in_specs=[pl.BlockSpec(memory_space=pltpu.HBM)] * 4,
        out_specs=(vmem(), vmem()),
        scratch_shapes=[
            pltpu.VMEM(queries.shape, bf16),
            pltpu.VMEM(cache.shape, bf16),
            pltpu.SemaphoreType.DMA((4,)),
        ],
        compiler_params=pltpu.CompilerParams(vmem_limit_bytes=VMEM_LIMIT),
        name="prepare",
    )(queries, cache, wk, wv)


def query_kernel(place, p0, p1, p2, p3, p4, q_out, wv_out, pieces, panel, values):
    me = place[0]
    sources = [
        (ref, i, lax.bitwise_xor(me, flip))
        for ref, flips in (
            (p0, (0,)),
            (p1, (8,)),
            (p2, (4, 12)),
            (p3, (2, 10, 6, 14)),
            (p4, (1, 9, 5, 13, 3, 11, 7, 15)),
        )
        for i, flip in enumerate(flips)
    ]
    for ref, i, src in sources:
        for k in range(6):
            pieces[k, src] = ref[i, TOK * k : TOK * (k + 1), :]
        for h in range(HEADS):
            panel[h, src] = ref[i, 96 + 32 * h : 128 + 32 * h, :]
            values[h, src] = ref[i, 224 + 32 * h : 256 + 32 * h, :]
    zero = jnp.zeros((ROWS, ROT), bf16)
    for h in range(HEADS):
        wv_out[h] = values[h].reshape(LATENT, VALUE)
        k = (h // 2) * 3
        tile = [pieces[k + n].reshape(ROWS, 128) for n in range(3)]
        if h % 2 == 0:
            plain, rot = tile[0], tile[1][:, :ROT]
        else:
            plain = jnp.concatenate([tile[1][:, ROT:], tile[2][:, :ROT]], axis=1)
            rot = tile[2][:, ROT:]
        lat = lax.dot_general(
            plain,
            panel[h].reshape(LATENT, PLAIN),
            (((1,), (1,)), ((), ())),
            preferred_element_type=f32,
        ).astype(bf16)
        for half in range(2):
            q_out[half, h, :, :LATENT] = lat
        q_out[0, h, :, LATENT:] = jnp.concatenate([rot, zero], axis=1)
        q_out[1, h, :, LATENT:] = jnp.concatenate([zero, rot], axis=1)


def split3(x):
    hi = x.astype(bf16)
    r = x - hi.astype(f32)
    mid = r.astype(bf16)
    lo = (r - mid.astype(f32)).astype(bf16)
    return hi, mid, lo


def pack_lse(columns, shape):
    lane = lax.broadcasted_iota(jnp.int32, shape, len(shape) - 1)
    tile = jnp.zeros(shape, f32)
    for h, column in enumerate(columns):
        for p, part in enumerate(split3(column)):
            tile = jnp.where(lane == 3 * h + p, part.astype(f32), tile)
    return tile.astype(bf16)


def lse_column(tile, h):
    t = tile.astype(f32)
    k = 3 * h
    return t[:, k : k + 1] + t[:, k + 1 : k + 2] + t[:, k + 2 : k + 3]


def attention_kernel(count, arrays, first, last, *refs):
    refs = list(refs)
    place, kpos, q = refs[:3]
    chunks = refs[3 : 3 + arrays]
    del refs[: 3 + arrays]
    if not first:
        acc_in, peak_in, total_in = refs[:3]
        del refs[:3]
    if last:
        wv = refs.pop(0)
        outs, (keys, parts) = refs[:4], refs[4:]
    else:
        acc_out, peak_out, total_out, keys = refs
    me, prior = place[0], place[1]

    for n, c in enumerate(chunks):
        shards = c.shape[0]
        start = n * 4 * 32 if shards == 4 else 0
        j = 0 if shards == 4 else n
        for half in range(2):
            keys[j, half, start : start + 32 * shards, :LATENT] = c[
                :, 32 * half : 32 * half + 32, :
            ].reshape(32 * shards, LATENT)
            for g in range(shards):
                for k in range(4):
                    at = start + 32 * g + 8 * k
                    keys[j, half, at : at + 8, LATENT:] = c[g, 64:72, 128 * k : 128 * (k + 1)]

    limit = prior + lax.broadcasted_iota(jnp.int32, (ROWS, 1), 0)
    blocks = [(j, half) for j in range(count) for half in range(2)]
    lses = []
    for h in range(HEADS):
        scores = []
        for n, (j, half) in enumerate(blocks):
            s = lax.dot_general(
                q[half, h], keys[j, half], (((1,), (1,)), ((), ())), preferred_element_type=f32
            )
            seen = kpos[:, 256 * n : 256 * (n + 1)] <= limit
            scores.append(jnp.where(seen, s * LOG2_SCALE, NEG))
        peak = scores[0].max(axis=1, keepdims=True)
        for s in scores[1:]:
            peak = jnp.maximum(peak, s.max(axis=1, keepdims=True))
        if first:
            total = jnp.zeros((ROWS, 1), f32)
            acc = jnp.zeros((ROWS, LATENT), f32)
        else:
            old = peak_in[h][:, :1]
            peak = jnp.maximum(peak, old)
            fade = jnp.exp2(old - peak)
            total = total_in[h][:, :1] * fade
            acc = acc_in[h] * fade
        for s, (j, half) in zip(scores, blocks):
            p = jnp.exp2(s - peak)
            total = total + p.sum(axis=1, keepdims=True)
            acc = acc + jnp.dot(
                p.astype(bf16), keys[j, half, :, :LATENT], preferred_element_type=f32
            )
        if not last:
            acc_out[h] = acc
            peak_out[h] = jnp.broadcast_to(peak, (ROWS, 128))
            total_out[h] = jnp.broadcast_to(total, (ROWS, 128))
            continue
        latent = (acc / total).astype(bf16)
        o = jnp.dot(latent, wv[h], preferred_element_type=f32).astype(bf16)
        for g in range(16):
            parts[g, h] = o[TOK * g : TOK * (g + 1)]
        lses.append(peak + jnp.log2(total))
    if last:
        tile = pack_lse(lses, (ROWS, 128))
        for g in range(16):
            parts[g, HEADS] = tile[TOK * g : TOK * (g + 1)]
        low = lax.bitwise_and(me, 3)
        for d in range(4):
            for high in range(4):
                outs[d][high] = parts[high * 4 + lax.bitwise_xor(low, d)]


def merge_heads(tiles):
    values, lses = [], []
    for h in range(HEADS):
        columns = [lse_column(t[HEADS], h) for t in tiles]
        top = columns[0]
        for c in columns[1:]:
            top = jnp.maximum(top, c)
        acc = jnp.zeros((TOK, VALUE), f32)
        total = jnp.zeros((TOK, 1), f32)
        for t, c in zip(tiles, columns):
            w = jnp.exp2(c - top)
            total = total + w
            acc = acc + t[h].astype(f32) * w
        values.append(acc / total)
        lses.append(top + jnp.log2(total))
    return values, lses


def middle_kernel(place, a, b, c, d, *outs):
    high = lax.shift_right_logical(place[0], 2)
    for j, out in enumerate(outs):
        g = lax.bitwise_xor(high, j)
        values, lses = merge_heads([r[g] for r in (a, b, c, d)])
        for h in range(HEADS):
            out[h] = values[h].astype(bf16)
        out[HEADS] = pack_lse(lses, (TOK, 128))


def final_kernel(place, a, b, c, d, out):
    values, _ = merge_heads([r[...] for r in (a, b, c, d)])
    for h in range(HEADS):
        out[:, h * VALUE : (h + 1) * VALUE] = values[h].astype(bf16)


def swap(x, axis, n, d):
    return lax.ppermute(x, axis, [(i, i ^ d) for i in range(n)])


def per_device(queries, cache, key_up_weight, value_up_weight, prior_len):
    zl, co = lax.axis_index("zl"), lax.axis_index("co")
    x, y, zh = lax.axis_index("x"), lax.axis_index("y"), lax.axis_index("zh")
    place = jnp.concatenate([(zl * 2 + co).astype(jnp.int32)[None], prior_len])

    shard, pack = prepare(
        queries,
        cache,
        key_up_weight.transpose(0, 2, 1).reshape(128, 128),
        value_up_weight.transpose(0, 2, 1).reshape(128, 128),
    )

    pieces = [pack]

    def widen(pack, d):
        got = swap(pack, CTX, 16, d)
        pieces.append(got)
        return jnp.concatenate([pack, got], axis=0)

    mirror = lax.ppermute(shard, ("zl", "zh"), [(i, 15 - i) for i in range(16)])
    pack = widen(pack, 8)
    mirror, pack = lax.optimization_barrier((mirror, pack))
    pair = jnp.concatenate([shard, mirror], axis=0)
    quad = jnp.concatenate([pair] + [swap(pair, "x", 4, d) for d in (1, 2, 3)], axis=0)
    pack = widen(pack, 4)
    quad, pack = lax.optimization_barrier((quad, pack))
    near, back = swap(quad, "y", 4, 1), swap(quad, "y", 4, 3)
    pack = widen(pack, 2)
    near, back, pack = lax.optimization_barrier((near, back, pack))
    far = (swap(near[:4], "y", 4, 3), swap(back[4:], "y", 4, 1))
    pieces.append(swap(pack, CTX, 16, 1))

    q, wv = call(
        query_kernel,
        (shaped((2, HEADS, ROWS, WIDE)), shaped((HEADS, LATENT, VALUE))),
        5,
        "query",
        (
            pltpu.VMEM((6, 16, TOK, 128), bf16),
            pltpu.VMEM((HEADS, 16, 32, 128), bf16),
            pltpu.VMEM((HEADS, 16, 32, 128), bf16),
        ),
    )(place, *pieces)

    n = jnp.arange(2048, dtype=jnp.int32)
    dy, half, dx, m, i = n >> 9, (n >> 8) & 1, (n >> 6) & 3, (n >> 5) & 1, n & 31
    dy = jnp.where(dy < 2, dy, 5 - dy)
    src_z, src_h = jnp.where(m == 1, 7 - zl, zl), jnp.where(m == 1, 1 - zh, zh)
    head = ((x ^ dx) * 4 + (y ^ dy)) * 2 + src_h
    kpos = (((src_z * 2 + co) * 32 + head) * 64 + half * 32 + i).astype(jnp.int32)[None]

    state = (
        shaped((HEADS, ROWS, LATENT), f32),
        shaped((HEADS, ROWS, 128), f32),
        shaped((HEADS, ROWS, 128), f32),
    )

    def attend(count, arrays, first, last, *operands):
        def kernel(*refs):
            attention_kernel(count, arrays, first, last, *refs)

        shape = state if not last else tuple(shaped((4, HEADS + 1, TOK, 128)) for _ in range(4))
        scratch = [pltpu.VMEM((count, 2, 256, WIDE), bf16)]
        if last:
            scratch.append(pltpu.VMEM((16, HEADS + 1, TOK, 128), bf16))
        return call(kernel, shape, len(operands) - 1, f"attend{count}{int(last)}", scratch)(*operands)

    run = attend(1, 1, True, False, place, kpos[:, :512], q, quad)
    run = attend(2, 2, False, False, place, kpos[:, 512:1536], q, near, back, *run)
    parts = attend(1, 2, False, True, place, kpos[:, 1536:], q, *far, *run, wv)

    got = [parts[0]] + [swap(parts[d], CTX, 16, d) for d in (1, 2, 3)]
    parts = call(middle_kernel, tuple(shaped((HEADS + 1, TOK, 128)) for _ in range(4)), 4, "middle")(place, *got)
    got = [parts[0]] + [swap(parts[d], CTX, 16, 4 * d) for d in (1, 2, 3)]
    return call(final_kernel, shaped((TOK, HEADS * VALUE)), 4, "final")(place, *got)


def solution(mesh):
    fine = Mesh(mesh.devices.reshape(8, 2, 4, 4, 2), ("zl", "co", "x", "y", "zh"))
    head = ("x", "y", "zh")
    return jax.shard_map(
        per_device,
        mesh=fine,
        in_specs=(P(CTX, head), P(CTX + head, None), P(head, None, CTX), P(head, None, CTX), P()),
        out_specs=P(CTX, head),
        check_vma=False,
    )
```

```python
import math

import jax
import jax.numpy as jnp
from jax import lax
from jax.experimental import pallas as pl
from jax.experimental.pallas import tpu as pltpu
from jax.sharding import Mesh
from jax.sharding import PartitionSpec as P

PLAIN = 128
ROT = 64
LATENT = 512
VALUE = 128
HEADS = 4
WIDE = LATENT + 2 * ROT
TOK = 16
ROWS = 256
NEG = -1e30
LOG2_SCALE = (PLAIN + ROT) ** (-0.5) * math.log2(math.e)
VMEM_LIMIT = 40 * 1024 * 1024

CTX = ("zl", "co")
f32 = jnp.float32
bf16 = jnp.bfloat16


def vmem():
    return pl.BlockSpec(memory_space=pltpu.VMEM)


def call(kernel, shape, n_in, name, scratch=()):
    return pl.pallas_call(
        kernel,
        out_shape=shape,
        in_specs=[pl.BlockSpec(memory_space=pltpu.SMEM)] + [vmem()] * n_in,
        out_specs=jax.tree.map(lambda _: vmem(), shape),
        scratch_shapes=list(scratch),
        compiler_params=pltpu.CompilerParams(vmem_limit_bytes=VMEM_LIMIT),
        cost_estimate=pl.CostEstimate(flops=1, transcendentals=0, bytes_accessed=1),
        name=name,
    )


def shaped(shape, dtype=bf16):
    return jax.ShapeDtypeStruct(shape, dtype)


def prepare_kernel(queries_hbm, cache_hbm, wk_hbm, wv_hbm, shard, pack, queries, cache, sems):
    copies = [
        pltpu.make_async_copy(src, dst, sems.at[i])
        for i, (src, dst) in enumerate(
            (
                (cache_hbm, cache),
                (queries_hbm, queries),
                (wk_hbm, pack.at[0, 96:224, :]),
                (wv_hbm, pack.at[0, 224:352, :]),
            )
        )
    ]
    for c in copies:
        c.start()
    copies[0].wait()
    shard[0, :64, :] = cache[:, :LATENT]
    rot = cache[:, LATENT:]
    pairs = jnp.concatenate([rot[:32], rot[32:]], axis=1)
    for k in range(4):
        shard[0, 64:72, 128 * k : 128 * (k + 1)] = pairs[8 * k : 8 * (k + 1)]
    copies[1].wait()
    for k in range(6):
        pack[0, TOK * k : TOK * (k + 1), :] = queries[:, 128 * k : 128 * (k + 1)]
    copies[2].wait()
    copies[3].wait()


def prepare(queries, cache, wk, wv):
    return pl.pallas_call(
        prepare_kernel,
        out_shape=(shaped((1, 72, LATENT)), shaped((1, 352, 128))),
        in_specs=[pl.BlockSpec(memory_space=pltpu.HBM)] * 4,
        out_specs=(vmem(), vmem()),
        scratch_shapes=[
            pltpu.VMEM(queries.shape, bf16),
            pltpu.VMEM(cache.shape, bf16),
            pltpu.SemaphoreType.DMA((4,)),
        ],
        compiler_params=pltpu.CompilerParams(vmem_limit_bytes=VMEM_LIMIT),
        name="prepare",
    )(queries, cache, wk, wv)


def query_kernel(place, p0, p1, p2, p3, p4, q_out, wv_out, pieces, panel, values):
    me = place[0]
    sources = [
        (ref, i, lax.bitwise_xor(me, flip))
        for ref, flips in (
            (p0, (0,)),
            (p1, (8,)),
            (p2, (4, 12)),
            (p3, (2, 10, 6, 14)),
            (p4, (1, 9, 5, 13, 3, 11, 7, 15)),
        )
        for i, flip in enumerate(flips)
    ]
    for ref, i, src in sources:
        for k in range(6):
            pieces[k, src] = ref[i, TOK * k : TOK * (k + 1), :]
        for h in range(HEADS):
            panel[h, src] = ref[i, 96 + 32 * h : 128 + 32 * h, :]
            values[h, src] = ref[i, 224 + 32 * h : 256 + 32 * h, :]
    zero = jnp.zeros((ROWS, ROT), bf16)
    for h in range(HEADS):
        wv_out[h] = values[h].reshape(LATENT, VALUE)
        k = (h // 2) * 3
        tile = [pieces[k + n].reshape(ROWS, 128) for n in range(3)]
        if h % 2 == 0:
            plain, rot = tile[0], tile[1][:, :ROT]
        else:
            plain = jnp.concatenate([tile[1][:, ROT:], tile[2][:, :ROT]], axis=1)
            rot = tile[2][:, ROT:]
        lat = lax.dot_general(
            plain,
            panel[h].reshape(LATENT, PLAIN),
            (((1,), (1,)), ((), ())),
            preferred_element_type=f32,
        ).astype(bf16)
        for half in range(2):
            q_out[half, h, :, :LATENT] = lat
        q_out[0, h, :, LATENT:] = jnp.concatenate([rot, zero], axis=1)
        q_out[1, h, :, LATENT:] = jnp.concatenate([zero, rot], axis=1)


def split3(x):
    hi = x.astype(bf16)
    r = x - hi.astype(f32)
    mid = r.astype(bf16)
    lo = (r - mid.astype(f32)).astype(bf16)
    return hi, mid, lo


def pack_lse(columns, shape):
    lane = lax.broadcasted_iota(jnp.int32, shape, len(shape) - 1)
    tile = jnp.zeros(shape, f32)
    for h, column in enumerate(columns):
        for p, part in enumerate(split3(column)):
            tile = jnp.where(lane == 3 * h + p, part.astype(f32), tile)
    return tile.astype(bf16)


def lse_column(tile, h):
    t = tile.astype(f32)
    k = 3 * h
    return t[:, k : k + 1] + t[:, k + 1 : k + 2] + t[:, k + 2 : k + 3]


def attention_kernel(count, arrays, first, last, *refs):
    refs = list(refs)
    place, kpos, q = refs[:3]
    chunks = refs[3 : 3 + arrays]
    del refs[: 3 + arrays]
    if not first:
        acc_in, peak_in, total_in = refs[:3]
        del refs[:3]
    if last:
        wv = refs.pop(0)
        outs, (keys, parts) = refs[:2], refs[2:]
    else:
        acc_out, peak_out, total_out, keys = refs
    me, prior = place[0], place[1]

    for n, c in enumerate(chunks):
        shards = c.shape[0]
        start = n * 4 * 32 if shards == 4 else 0
        j = 0 if shards == 4 else n
        for half in range(2):
            keys[j, half, start : start + 32 * shards, :LATENT] = c[
                :, 32 * half : 32 * half + 32, :
            ].reshape(32 * shards, LATENT)
            for g in range(shards):
                for k in range(4):
                    at = start + 32 * g + 8 * k
                    keys[j, half, at : at + 8, LATENT:] = c[g, 64:72, 128 * k : 128 * (k + 1)]

    limit = prior + lax.broadcasted_iota(jnp.int32, (ROWS, 1), 0)
    blocks = [(j, half) for j in range(count) for half in range(2)]
    lses = []
    for h in range(HEADS):
        scores = []
        for n, (j, half) in enumerate(blocks):
            s = lax.dot_general(
                q[half, h], keys[j, half], (((1,), (1,)), ((), ())), preferred_element_type=f32
            )
            seen = kpos[:, 256 * n : 256 * (n + 1)] <= limit
            scores.append(jnp.where(seen, s * LOG2_SCALE, NEG))
        peak = scores[0].max(axis=1, keepdims=True)
        for s in scores[1:]:
            peak = jnp.maximum(peak, s.max(axis=1, keepdims=True))
        if first:
            total = jnp.zeros((ROWS, 1), f32)
            acc = jnp.zeros((ROWS, LATENT), f32)
        else:
            old = peak_in[h][:, :1]
            peak = jnp.maximum(peak, old)
            fade = jnp.exp2(old - peak)
            total = total_in[h][:, :1] * fade
            acc = acc_in[h] * fade
        for s, (j, half) in zip(scores, blocks):
            p = jnp.exp2(s - peak)
            total = total + p.sum(axis=1, keepdims=True)
            acc = acc + jnp.dot(
                p.astype(bf16), keys[j, half, :, :LATENT], preferred_element_type=f32
            )
        if not last:
            acc_out[h] = acc
            peak_out[h] = jnp.broadcast_to(peak, (ROWS, 128))
            total_out[h] = jnp.broadcast_to(total, (ROWS, 128))
            continue
        latent = (acc / total).astype(bf16)
        o = jnp.dot(latent, wv[h], preferred_element_type=f32).astype(bf16)
        for g in range(16):
            parts[g, h] = o[TOK * g : TOK * (g + 1)]
        lses.append(peak + jnp.log2(total))
    if last:
        tile = pack_lse(lses, (ROWS, 128))
        for g in range(16):
            parts[g, HEADS] = tile[TOK * g : TOK * (g + 1)]
        low = lax.bitwise_and(me, 1)
        for d in range(2):
            for zl in range(8):
                outs[d][zl] = parts[zl * 2 + lax.bitwise_xor(low, d)]


def merge_heads(tiles):
    values, lses = [], []
    for h in range(HEADS):
        columns = [lse_column(t[HEADS], h) for t in tiles]
        top = columns[0]
        for c in columns[1:]:
            top = jnp.maximum(top, c)
        acc = jnp.zeros((TOK, VALUE), f32)
        total = jnp.zeros((TOK, 1), f32)
        for t, c in zip(tiles, columns):
            w = jnp.exp2(c - top)
            total = total + w
            acc = acc + t[h].astype(f32) * w
        values.append(acc / total)
        lses.append(top + jnp.log2(total))
    return values, lses


def pair_kernel(place, a, b, out):
    for g in range(8):
        values, lses = merge_heads([a[g], b[g]])
        for h in range(HEADS):
            out[g, h] = values[h].astype(bf16)
        out[g, HEADS] = pack_lse(lses, (TOK, 128))


def final_kernel(place, x, out):
    values, _ = merge_heads([x[g] for g in range(8)])
    for h in range(HEADS):
        out[:, h * VALUE : (h + 1) * VALUE] = values[h].astype(bf16)


def swap(x, axis, n, d):
    return lax.ppermute(x, axis, [(i, i ^ d) for i in range(n)])


def per_device(queries, cache, key_up_weight, value_up_weight, prior_len):
    zl, co = lax.axis_index("zl"), lax.axis_index("co")
    x, y, zh = lax.axis_index("x"), lax.axis_index("y"), lax.axis_index("zh")
    place = jnp.concatenate([(zl * 2 + co).astype(jnp.int32)[None], prior_len])

    shard, pack = prepare(
        queries,
        cache,
        key_up_weight.transpose(0, 2, 1).reshape(128, 128),
        value_up_weight.transpose(0, 2, 1).reshape(128, 128),
    )

    pieces = [pack]

    def widen(pack, d):
        got = swap(pack, CTX, 16, d)
        pieces.append(got)
        return jnp.concatenate([pack, got], axis=0)

    mirror = lax.ppermute(shard, ("zl", "zh"), [(i, 15 - i) for i in range(16)])
    pack = widen(pack, 8)
    mirror, pack = lax.optimization_barrier((mirror, pack))
    pair = jnp.concatenate([shard, mirror], axis=0)
    sides = [swap(pair, "x", 4, d) for d in (1, 2, 3)]
    pack = widen(pack, 4)
    *sides, _ = lax.optimization_barrier((*sides, pack))
    quad = jnp.concatenate([pair] + sides, axis=0)
    near, back = swap(quad, "y", 4, 1), swap(quad, "y", 4, 3)
    pack = widen(pack, 2)
    near, back, _ = lax.optimization_barrier((near, back, pack))
    far = (swap(near[:4], "y", 4, 3), swap(back[4:], "y", 4, 1))
    pieces.append(swap(pack, CTX, 16, 1))

    q, wv = call(
        query_kernel,
        (shaped((2, HEADS, ROWS, WIDE)), shaped((HEADS, LATENT, VALUE))),
        5,
        "query",
        (
            pltpu.VMEM((6, 16, TOK, 128), bf16),
            pltpu.VMEM((HEADS, 16, 32, 128), bf16),
            pltpu.VMEM((HEADS, 16, 32, 128), bf16),
        ),
    )(place, *pieces)

    n = jnp.arange(2048, dtype=jnp.int32)
    dy, half, dx, m, i = n >> 9, (n >> 8) & 1, (n >> 6) & 3, (n >> 5) & 1, n & 31
    dy = jnp.where(dy < 2, dy, 5 - dy)
    src_z, src_h = jnp.where(m == 1, 7 - zl, zl), jnp.where(m == 1, 1 - zh, zh)
    head = ((x ^ dx) * 4 + (y ^ dy)) * 2 + src_h
    kpos = (((src_z * 2 + co) * 32 + head) * 64 + half * 32 + i).astype(jnp.int32)[None]

    state = (
        shaped((HEADS, ROWS, LATENT), f32),
        shaped((HEADS, ROWS, 128), f32),
        shaped((HEADS, ROWS, 128), f32),
    )

    def attend(count, arrays, first, last, *operands):
        def kernel(*refs):
            attention_kernel(count, arrays, first, last, *refs)

        shape = state if not last else (shaped((8, HEADS + 1, TOK, 128)),) * 2
        scratch = [pltpu.VMEM((count, 2, 256, WIDE), bf16)]
        if last:
            scratch.append(pltpu.VMEM((16, HEADS + 1, TOK, 128), bf16))
        return call(kernel, shape, len(operands) - 1, f"attend{count}{int(last)}", scratch)(*operands)

    run = attend(1, 1, True, False, place, kpos[:, :512], q, quad)
    run = attend(2, 2, False, False, place, kpos[:, 512:1536], q, near, back, *run)
    parts = attend(1, 2, False, True, place, kpos[:, 1536:], q, *far, *run, wv)

    merged = call(pair_kernel, shaped((8, HEADS + 1, TOK, 128)), 2, "pair")(
        place, parts[0], swap(parts[1], CTX, 16, 1)
    )
    spread = lax.all_to_all(merged, "zl", 0, 0, tiled=True)
    return call(final_kernel, shaped((TOK, HEADS * VALUE)), 1, "final")(place, spread)


def solution(mesh):
    fine = Mesh(mesh.devices.reshape(8, 2, 4, 4, 2), ("zl", "co", "x", "y", "zh"))
    head = ("x", "y", "zh")
    return jax.shard_map(
        per_device,
        mesh=fine,
        in_specs=(P(CTX, head), P(CTX + head, None), P(head, None, CTX), P(head, None, CTX), P()),
        out_specs=P(CTX, head),
        check_vma=False,
    )
```

```python
import math

import jax
import jax.numpy as jnp
from jax import lax
from jax.experimental import pallas as pl
from jax.experimental.pallas import tpu as pltpu
from jax.sharding import Mesh
from jax.sharding import PartitionSpec as P

PLAIN = 128
ROT = 64
LATENT = 512
VALUE = 128
HEADS = 4
WIDE = LATENT + 2 * ROT
TOK = 16
ROWS = 256
NEG = -1e30
LOG2_SCALE = (PLAIN + ROT) ** (-0.5) * math.log2(math.e)
VMEM_LIMIT = 40 * 1024 * 1024

ZL = ("zq", "zr")
CTX = ("zq", "zr", "co")
f32 = jnp.float32
bf16 = jnp.bfloat16


def vmem():
    return pl.BlockSpec(memory_space=pltpu.VMEM)


def call(kernel, shape, n_in, name, scratch=()):
    return pl.pallas_call(
        kernel,
        out_shape=shape,
        in_specs=[pl.BlockSpec(memory_space=pltpu.SMEM)] + [vmem()] * n_in,
        out_specs=jax.tree.map(lambda _: vmem(), shape),
        scratch_shapes=list(scratch),
        compiler_params=pltpu.CompilerParams(vmem_limit_bytes=VMEM_LIMIT),
        cost_estimate=pl.CostEstimate(flops=1, transcendentals=0, bytes_accessed=1),
        name=name,
    )


def shaped(shape, dtype=bf16):
    return jax.ShapeDtypeStruct(shape, dtype)


def prepare_kernel(queries_hbm, cache_hbm, wk_hbm, wv_hbm, shard, pack, queries, cache, sems):
    copies = [
        pltpu.make_async_copy(src, dst, sems.at[i])
        for i, (src, dst) in enumerate(
            (
                (cache_hbm, cache),
                (queries_hbm, queries),
                (wk_hbm, pack.at[0, 96:224, :]),
                (wv_hbm, pack.at[0, 224:352, :]),
            )
        )
    ]
    for c in copies:
        c.start()
    copies[0].wait()
    shard[0, :64, :] = cache[:, :LATENT]
    rot = cache[:, LATENT:]
    pairs = jnp.concatenate([rot[:32], rot[32:]], axis=1)
    for k in range(4):
        shard[0, 64:72, 128 * k : 128 * (k + 1)] = pairs[8 * k : 8 * (k + 1)]
    copies[1].wait()
    for k in range(6):
        pack[0, TOK * k : TOK * (k + 1), :] = queries[:, 128 * k : 128 * (k + 1)]
    copies[2].wait()
    copies[3].wait()


def prepare(queries, cache, wk, wv):
    return pl.pallas_call(
        prepare_kernel,
        out_shape=(shaped((1, 72, LATENT)), shaped((1, 352, 128))),
        in_specs=[pl.BlockSpec(memory_space=pltpu.HBM)] * 4,
        out_specs=(vmem(), vmem()),
        scratch_shapes=[
            pltpu.VMEM(queries.shape, bf16),
            pltpu.VMEM(cache.shape, bf16),
            pltpu.SemaphoreType.DMA((4,)),
        ],
        compiler_params=pltpu.CompilerParams(vmem_limit_bytes=VMEM_LIMIT),
        name="prepare",
    )(*(pltpu.with_memory_space_constraint(v, pltpu.HBM) for v in (queries, cache, wk, wv)))


def query_kernel(place, p0, p1, p2, p3, p4, q_out, wv_out, pieces, panel):
    me = place[0]
    sources = [
        (ref, i, lax.bitwise_xor(me, flip))
        for ref, flips in (
            (p0, (0, 8)),
            (p1, (2, 10)),
            (p2, (4, 12)),
            (p3, (6, 14)),
            (p4, (1, 9, 3, 11, 5, 13, 7, 15)),
        )
        for i, flip in enumerate(flips)
    ]
    for ref, i, src in sources:
        for k in range(6):
            pieces[k, src] = ref[i, TOK * k : TOK * (k + 1), :]
        for h in range(HEADS):
            panel[h, src] = ref[i, 96 + 32 * h : 128 + 32 * h, :]
            wv_out[h, src] = ref[i, 224 + 32 * h : 256 + 32 * h, :]
    zero = jnp.zeros((ROWS, ROT), bf16)
    for h in range(HEADS):
        k = (h // 2) * 3
        tile = [pieces[k + n].reshape(ROWS, 128) for n in range(3)]
        if h % 2 == 0:
            plain, rot = tile[0], tile[1][:, :ROT]
        else:
            plain = jnp.concatenate([tile[1][:, ROT:], tile[2][:, :ROT]], axis=1)
            rot = tile[2][:, ROT:]
        lat = lax.dot_general(
            plain,
            panel[h].reshape(LATENT, PLAIN),
            (((1,), (1,)), ((), ())),
            preferred_element_type=f32,
        ).astype(bf16)
        for half in range(2):
            q_out[half, h, :, :LATENT] = lat
        q_out[0, h, :, LATENT:] = jnp.concatenate([rot, zero], axis=1)
        q_out[1, h, :, LATENT:] = jnp.concatenate([zero, rot], axis=1)


def split3(x):
    hi = x.astype(bf16)
    r = x - hi.astype(f32)
    mid = r.astype(bf16)
    lo = (r - mid.astype(f32)).astype(bf16)
    return hi, mid, lo


def pack_lse(columns, shape):
    lane = lax.broadcasted_iota(jnp.int32, shape, len(shape) - 1)
    tile = jnp.zeros(shape, f32)
    for h, column in enumerate(columns):
        for p, part in enumerate(split3(column)):
            tile = jnp.where(lane == 3 * h + p, part.astype(f32), tile)
    return tile.astype(bf16)


def lse_column(tile, h):
    t = tile.astype(f32)
    k = 3 * h
    return t[..., k : k + 1] + t[..., k + 1 : k + 2] + t[..., k + 2 : k + 3]


def attention_kernel(last, place, q, chunk, *refs):
    me, zh, prior = place[0], place[1], place[2]
    zl, co = lax.shift_right_logical(me, 1), lax.bitwise_and(me, 1)
    if last:
        acc_in, peak_in, total_in, values, keep, send, keys, parts = refs
        zl, zh = 7 - zl, 1 - zh
    else:
        acc_out, peak_out, total_out, keys = refs

    for half in range(2):
        keys[half, :, :LATENT] = chunk[:, 32 * half : 32 * half + 32, :].reshape(512, LATENT)
        for g in range(16):
            for k in range(4):
                at = 32 * g + 8 * k
                keys[half, at : at + 8, LATENT:] = chunk[g, 64:72, 128 * k : 128 * (k + 1)]

    limit = prior + lax.broadcasted_iota(jnp.int32, (ROWS, 1), 0)
    n = lax.broadcasted_iota(jnp.int32, (1, 512), 1)
    slot = ((zl * 2 + co) * 32 + zh) * 64 + lax.shift_right_logical(n, 5) * 128 + lax.bitwise_and(n, 31)
    lses = []
    for h in range(HEADS):
        scores = []
        for half in range(2):
            s = lax.dot_general(
                q[half, h], keys[half], (((1,), (1,)), ((), ())), preferred_element_type=f32
            )
            scores.append(jnp.where(slot + 32 * half <= limit, s * LOG2_SCALE, NEG))
        peak = jnp.maximum(scores[0], scores[1]).max(axis=1, keepdims=True)
        if last:
            old = peak_in[h][:, :1]
            peak = jnp.maximum(peak, old)
            fade = jnp.exp2(old - peak)
            total = total_in[h][:, :1] * fade
            acc = acc_in[h] * fade
        else:
            total = jnp.zeros((ROWS, 1), f32)
            acc = jnp.zeros((ROWS, LATENT), f32)
        for half in range(2):
            p = jnp.exp2(scores[half] - peak)
            total = total + p.sum(axis=1, keepdims=True)
            acc = acc + jnp.dot(p.astype(bf16), keys[half, :, :LATENT], preferred_element_type=f32)
        if not last:
            acc_out[h] = acc
            peak_out[h] = jnp.broadcast_to(peak, (ROWS, 128))
            total_out[h] = jnp.broadcast_to(total, (ROWS, 128))
            continue
        latent = (acc / total).astype(bf16)
        o = jnp.dot(latent, values[h].reshape(LATENT, VALUE), preferred_element_type=f32).astype(bf16)
        for g in range(16):
            parts[g, h] = o[TOK * g : TOK * (g + 1)]
        lses.append(peak + jnp.log2(total))
    if last:
        tile = pack_lse(lses, (ROWS, 128))
        for g in range(16):
            parts[g, HEADS] = tile[TOK * g : TOK * (g + 1)]
        for g in range(8):
            keep[g] = parts[g * 2 + co]
            send[g] = parts[g * 2 + 1 - co]


def merge_heads(blocks):
    tile = blocks[HEADS]
    values, lses = [], []
    for h in range(HEADS):
        column = lse_column(tile, h)
        top = column.max(axis=0)
        w = jnp.exp2(column - top)
        total = w.sum(axis=0)
        values.append((blocks[h].astype(f32) * w).sum(axis=0) / total)
        lses.append(top + jnp.log2(total))
    return values, lses


def pair_kernel(place, a, b, out):
    rows = 8 * TOK
    blocks = [
        jnp.concatenate([r[:, h].reshape(1, rows, 128) for r in (a, b)], axis=0)
        for h in range(HEADS + 1)
    ]
    values, lses = merge_heads(blocks)
    for h in range(HEADS):
        out[:, h] = values[h].astype(bf16).reshape(8, TOK, 128)
    out[:, HEADS] = pack_lse(lses, (rows, 128)).reshape(8, TOK, 128)


def final_kernel(place, x, out):
    values, _ = merge_heads([x[:, h] for h in range(HEADS + 1)])
    for h in range(HEADS):
        out[:, h * VALUE : (h + 1) * VALUE] = values[h].astype(bf16)


def swap(x, d):
    return lax.ppermute(x, CTX, [(i, i ^ d) for i in range(16)])


def gather(x, axes, n):
    copies = jnp.broadcast_to(x[None], (n, *x.shape)).reshape(n * x.shape[0], *x.shape[1:])
    return lax.all_to_all(copies, axes, 0, 0, tiled=True)


def per_device(queries, cache, key_up_weight, value_up_weight, prior_len):
    me, zh = lax.axis_index(CTX), lax.axis_index("zh")
    place = jnp.concatenate([jnp.stack([me, zh]).astype(jnp.int32), prior_len])

    shard, pack = prepare(
        queries,
        cache,
        key_up_weight.transpose(0, 2, 1).reshape(128, 128),
        value_up_weight.transpose(0, 2, 1).reshape(128, 128),
    )

    mirror = lax.ppermute(shard, ("zq", "zr", "zh"), [(i, 15 - i) for i in range(16)])
    here = gather(shard, ("x", "y"), 16)
    pack2 = jnp.concatenate([pack, swap(pack, 8)], axis=0)
    mirror, later = lax.optimization_barrier((mirror, pack2))
    fans = [swap(later, 2), swap(later, 4), swap(later, 6)]
    mirror, here = lax.optimization_barrier((mirror, here))
    there = gather(mirror, ("x", "y"), 16)
    pack8 = jnp.concatenate([pack2] + fans, axis=0)


    q, wv = call(
        query_kernel,
        (shaped((2, HEADS, ROWS, WIDE)), shaped((HEADS, 16, 32, 128))),
        5,
        "query",
        (pltpu.VMEM((6, 16, TOK, 128), bf16), pltpu.VMEM((HEADS, 16, 32, 128), bf16)),
    )(place, pack2, *fans, swap(pack8, 1))

    def attend(last, shape, scratch, *operands):
        def kernel(*refs):
            attention_kernel(last, *refs)

        scratch = (pltpu.VMEM((2, 512, WIDE), bf16), *scratch)
        return call(kernel, shape, len(operands), f"attend{int(last)}", scratch)(place, *operands)

    state = (
        shaped((HEADS, ROWS, LATENT), f32),
        shaped((HEADS, ROWS, 128), f32),
        shaped((HEADS, ROWS, 128), f32),
    )
    run = attend(False, state, (), q, here)
    keep, send = attend(
        True,
        (shaped((8, HEADS + 1, TOK, 128)),) * 2,
        (pltpu.VMEM((16, HEADS + 1, TOK, 128), bf16),),
        q,
        there,
        *run,
        wv,
    )
    merged = call(pair_kernel, shaped((8, HEADS + 1, TOK, 128)), 2, "pair")(place, keep, swap(send, 1))
    spread = lax.all_to_all(merged, ZL, 0, 0, tiled=True)
    return call(final_kernel, shaped((TOK, HEADS * VALUE)), 1, "final")(place, spread)


def solution(mesh):
    fine = Mesh(mesh.devices.reshape(2, 4, 2, 4, 4, 2), ("zq", "zr", "co", "x", "y", "zh"))
    head = ("x", "y", "zh")
    return jax.shard_map(
        per_device,
        mesh=fine,
        in_specs=(P(CTX, head), P(CTX + head, None), P(head, None, CTX), P(head, None, CTX), P()),
        out_specs=P(CTX, head),
        check_vma=False,
    )
```

```python
import math

import jax
import jax.numpy as jnp
from jax import lax
from jax.experimental import pallas as pl
from jax.experimental.pallas import tpu as pltpu
from jax.sharding import Mesh
from jax.sharding import PartitionSpec as P

PLAIN = 128
ROT = 64
LATENT = 512
VALUE = 128
HEADS = 4
WIDE = LATENT + 2 * ROT
TOK = 16
ROWS = 256
NEG = -1e30
LOG2_SCALE = (PLAIN + ROT) ** (-0.5) * math.log2(math.e)
SLOTS = 1024
MIB = 1024 * 1024

ZL = ("zq", "zr")
CTX = ("zq", "zr", "co")
f32 = jnp.float32
bf16 = jnp.bfloat16


def vmem():
    return pl.BlockSpec(memory_space=pltpu.VMEM)


def call(kernel, shape, n_in, name, scratch=(), room=8):
    return pl.pallas_call(
        kernel,
        out_shape=shape,
        in_specs=[pl.BlockSpec(memory_space=pltpu.SMEM)] + [vmem()] * n_in,
        out_specs=jax.tree.map(lambda _: vmem(), shape),
        scratch_shapes=list(scratch),
        compiler_params=pltpu.CompilerParams(vmem_limit_bytes=room * MIB),
        cost_estimate=pl.CostEstimate(flops=1, transcendentals=0, bytes_accessed=1),
        name=name,
    )


def shaped(shape, dtype=bf16):
    return jax.ShapeDtypeStruct(shape, dtype)


def prepare_kernel(queries_hbm, cache_hbm, wk_hbm, wv_hbm, shard, pack, queries, cache, sems):
    copies = [
        pltpu.make_async_copy(src, dst, sems.at[i])
        for i, (src, dst) in enumerate(
            (
                (cache_hbm, cache),
                (queries_hbm, queries),
                (wk_hbm, pack.at[0, 96:224, :]),
                (wv_hbm, pack.at[0, 224:352, :]),
            )
        )
    ]
    for c in copies:
        c.start()
    copies[0].wait()
    shard[0, :64, :] = cache[:, :LATENT]
    rot = cache[:, LATENT:]
    pairs = jnp.concatenate([rot[:32], rot[32:]], axis=1)
    for k in range(4):
        shard[0, 64:72, 128 * k : 128 * (k + 1)] = pairs[8 * k : 8 * (k + 1)]
    copies[1].wait()
    for k in range(6):
        pack[0, TOK * k : TOK * (k + 1), :] = queries[:, 128 * k : 128 * (k + 1)]
    copies[2].wait()
    copies[3].wait()


def prepare(queries, cache, wk, wv):
    return pl.pallas_call(
        prepare_kernel,
        out_shape=(shaped((1, 72, LATENT)), shaped((1, 352, 128))),
        in_specs=[pl.BlockSpec(memory_space=pltpu.HBM)] * 4,
        out_specs=(vmem(), vmem()),
        scratch_shapes=[
            pltpu.VMEM(queries.shape, bf16),
            pltpu.VMEM(cache.shape, bf16),
            pltpu.SemaphoreType.DMA((4,)),
        ],
        compiler_params=pltpu.CompilerParams(vmem_limit_bytes=4 * MIB),
        name="prepare",
    )(*(pltpu.with_memory_space_constraint(v, pltpu.HBM) for v in (queries, cache, wk, wv)))


def query_kernel(place, *refs):
    inputs, (lat_out, rot_out, wv_out), (tiles, pieces, panel, lats, rots, values, sems) = (
        refs[:5],
        refs[5:8],
        refs[8:],
    )
    flips = ((0, 8), (2, 10), (4, 12), (6, 14), (1, 9, 3, 11, 5, 13, 7, 15))
    starts = (0, 2, 4, 6, 8)
    loads = [
        pltpu.make_async_copy(ref, tiles.at[at : at + len(f)], sems.at[n])
        for n, (ref, at, f) in enumerate(zip(inputs, starts, flips))
    ]
    for c in loads:
        c.start()
    for c, at, flip in zip(loads, starts, flips):
        c.wait()
        for i, d in enumerate(flip):
            src = lax.bitwise_xor(place[0], d)
            for k in range(6):
                pieces[k, src] = tiles[at + i, TOK * k : TOK * (k + 1), :]
            for h in range(HEADS):
                panel[h, src] = tiles[at + i, 96 + 32 * h : 128 + 32 * h, :]
                values[h, src] = tiles[at + i, 224 + 32 * h : 256 + 32 * h, :]
    stores = [pltpu.make_async_copy(values, wv_out, sems.at[5])]
    stores[0].start()
    zero = jnp.zeros((ROWS, ROT), bf16)
    for h in range(HEADS):
        k = (h // 2) * 3
        tile = [pieces[k + n].reshape(ROWS, 128) for n in range(3)]
        if h % 2 == 0:
            plain, rot = tile[0], tile[1][:, :ROT]
        else:
            plain = jnp.concatenate([tile[1][:, ROT:], tile[2][:, :ROT]], axis=1)
            rot = tile[2][:, ROT:]
        rots[0, h] = jnp.concatenate([rot, zero], axis=1)
        rots[1, h] = jnp.concatenate([zero, rot], axis=1)
        lats[h] = lax.dot_general(
            plain,
            panel[h].reshape(LATENT, PLAIN),
            (((1,), (1,)), ((), ())),
            preferred_element_type=f32,
        ).astype(bf16)
        stores.append(pltpu.make_async_copy(lats.at[h], lat_out.at[h], sems.at[6 + h]))
        stores[-1].start()
    stores.append(pltpu.make_async_copy(rots, rot_out, sems.at[10]))
    stores[-1].start()
    for c in stores:
        c.wait()


def project_queries(place, *pieces):
    hbm = pl.BlockSpec(memory_space=pltpu.HBM)
    return pl.pallas_call(
        query_kernel,
        out_shape=(
            pltpu.HBM((HEADS, ROWS, LATENT), bf16),
            pltpu.HBM((2, HEADS, ROWS, 2 * ROT), bf16),
            pltpu.HBM((HEADS, 16, 32, 128), bf16),
        ),
        in_specs=[pl.BlockSpec(memory_space=pltpu.SMEM)] + [hbm] * 5,
        out_specs=(hbm,) * 3,
        scratch_shapes=[
            pltpu.VMEM((16, 352, 128), bf16),
            pltpu.VMEM((6, 16, TOK, 128), bf16),
            pltpu.VMEM((HEADS, 16, 32, 128), bf16),
            pltpu.VMEM((HEADS, ROWS, LATENT), bf16),
            pltpu.VMEM((2, HEADS, ROWS, 2 * ROT), bf16),
            pltpu.VMEM((HEADS, 16, 32, 128), bf16),
            pltpu.SemaphoreType.DMA((11,)),
        ],
        compiler_params=pltpu.CompilerParams(vmem_limit_bytes=16 * MIB),
        name="query",
    )(place, *(pltpu.with_memory_space_constraint(p, pltpu.HBM) for p in pieces))


def split3(x):
    hi = x.astype(bf16)
    r = x - hi.astype(f32)
    mid = r.astype(bf16)
    lo = (r - mid.astype(f32)).astype(bf16)
    return hi, mid, lo


def pack_lse(columns, shape):
    lane = lax.broadcasted_iota(jnp.int32, shape, len(shape) - 1)
    tile = jnp.zeros(shape, f32)
    for h, column in enumerate(columns):
        for p, part in enumerate(split3(column)):
            tile = jnp.where(lane == 3 * h + p, part.astype(f32), tile)
    return tile.astype(bf16)


def lse_column(tile, h):
    t = tile.astype(f32)
    k = 3 * h
    return t[..., k : k + 1] + t[..., k + 1 : k + 2] + t[..., k + 2 : k + 3]


def attention_kernel(place, lat_hbm, rot_hbm, wv_hbm, chunk, keep, send, keys, parts, lats, rots, values, sems):
    me, zh, prior = place[0], place[1], place[2]
    zl, co = lax.shift_right_logical(me, 1), lax.bitwise_and(me, 1)
    loads = [
        pltpu.make_async_copy(rot_hbm, rots, sems.at[0]),
        *(pltpu.make_async_copy(lat_hbm.at[h], lats.at[h], sems.at[1 + h]) for h in range(HEADS)),
        pltpu.make_async_copy(wv_hbm, values, sems.at[1 + HEADS]),
    ]
    for c in loads:
        c.start()
    for half in range(2):
        keys[half, :, :LATENT] = chunk[:, 32 * half : 32 * half + 32, :].reshape(SLOTS, LATENT)
        for g in range(32):
            for k in range(4):
                at = 32 * g + 8 * k
                keys[half, at : at + 8, LATENT:] = chunk[g, 64:72, 128 * k : 128 * (k + 1)]

    limit = prior + lax.broadcasted_iota(jnp.int32, (ROWS, 1), 0)
    n = lax.broadcasted_iota(jnp.int32, (1, SLOTS), 1)
    near = ((zl * 2 + co) * 32 + zh) * 64
    far = (((7 - zl) * 2 + co) * 32 + 1 - zh) * 64
    slot = lax.shift_right_logical(n, 6) * 128 + lax.bitwise_and(n, 31)
    slot = slot + jnp.where(lax.bitwise_and(n, 32) == 0, near, far)
    lses = []
    loads[0].wait()
    for h in range(HEADS):
        loads[1 + h].wait()
        scores = []
        for half in range(2):
            q = jnp.concatenate([lats[h], rots[half, h]], axis=1)
            s = lax.dot_general(
                q, keys[half], (((1,), (1,)), ((), ())), preferred_element_type=f32
            )
            scores.append(jnp.where(slot + 32 * half <= limit, s * LOG2_SCALE, NEG))
        peak = jnp.maximum(scores[0], scores[1]).max(axis=1, keepdims=True)
        total = jnp.zeros((ROWS, 1), f32)
        acc = jnp.zeros((ROWS, LATENT), f32)
        for half in range(2):
            p = jnp.exp2(scores[half] - peak)
            total = total + p.sum(axis=1, keepdims=True)
            acc = acc + jnp.dot(p.astype(bf16), keys[half, :, :LATENT], preferred_element_type=f32)
        if h == 0:
            loads[1 + HEADS].wait()
        latent = (acc / total).astype(bf16)
        o = jnp.dot(latent, values[h].reshape(LATENT, VALUE), preferred_element_type=f32).astype(bf16)
        for g in range(16):
            parts[g, h] = o[TOK * g : TOK * (g + 1)]
        lses.append(peak + jnp.log2(total))
    tile = pack_lse(lses, (ROWS, 128))
    for g in range(16):
        parts[g, HEADS] = tile[TOK * g : TOK * (g + 1)]
    for g in range(8):
        keep[g] = parts[g * 2 + co]
        send[g] = parts[g * 2 + 1 - co]


def attend(place, lat, rot, wv, slots):
    hbm = pl.BlockSpec(memory_space=pltpu.HBM)
    return pl.pallas_call(
        attention_kernel,
        out_shape=(shaped((8, HEADS + 1, TOK, 128)),) * 2,
        in_specs=[pl.BlockSpec(memory_space=pltpu.SMEM)] + [hbm] * 3 + [vmem()],
        out_specs=(vmem(), vmem()),
        scratch_shapes=[
            pltpu.VMEM((2, SLOTS, WIDE), bf16),
            pltpu.VMEM((16, HEADS + 1, TOK, 128), bf16),
            pltpu.VMEM(lat.shape, bf16),
            pltpu.VMEM(rot.shape, bf16),
            pltpu.VMEM(wv.shape, bf16),
            pltpu.SemaphoreType.DMA((2 + HEADS,)),
        ],
        compiler_params=pltpu.CompilerParams(vmem_limit_bytes=24 * MIB),
        name="attention",
    )(place, *(pltpu.with_memory_space_constraint(v, pltpu.HBM) for v in (lat, rot, wv)), slots)


def merge_heads(blocks):
    tile = blocks[HEADS]
    values, lses = [], []
    for h in range(HEADS):
        column = lse_column(tile, h)
        top = column.max(axis=0)
        w = jnp.exp2(column - top)
        total = w.sum(axis=0)
        values.append((blocks[h].astype(f32) * w).sum(axis=0) / total)
        lses.append(top + jnp.log2(total))
    return values, lses


def pair_kernel(place, a, b, out):
    rows = 8 * TOK
    blocks = [
        jnp.concatenate([r[:, h].reshape(1, rows, 128) for r in (a, b)], axis=0)
        for h in range(HEADS + 1)
    ]
    values, lses = merge_heads(blocks)
    for h in range(HEADS):
        out[:, h] = values[h].astype(bf16).reshape(8, TOK, 128)
    out[:, HEADS] = pack_lse(lses, (rows, 128)).reshape(8, TOK, 128)


def final_kernel(place, x, out):
    values, _ = merge_heads([x[:, h] for h in range(HEADS + 1)])
    for h in range(HEADS):
        out[:, h * VALUE : (h + 1) * VALUE] = values[h].astype(bf16)


def swap(x, d):
    return lax.ppermute(x, CTX, [(i, i ^ d) for i in range(16)])


def gather(x, axes, n):
    copies = jnp.broadcast_to(x[None], (n, *x.shape)).reshape(n * x.shape[0], *x.shape[1:])
    return lax.all_to_all(copies, axes, 0, 0, tiled=True)


def per_device(queries, cache, key_up_weight, value_up_weight, prior_len):
    me, zh = lax.axis_index(CTX), lax.axis_index("zh")
    place = jnp.concatenate([jnp.stack([me, zh]).astype(jnp.int32), prior_len])

    shard, pack = prepare(
        queries,
        cache,
        key_up_weight.transpose(0, 2, 1).reshape(128, 128),
        value_up_weight.transpose(0, 2, 1).reshape(128, 128),
    )

    mirror = lax.ppermute(shard, ("zq", "zr", "zh"), [(i, 15 - i) for i in range(16)])
    pack2 = jnp.concatenate([pack, swap(pack, 8)], axis=0)
    mirror, pack2 = lax.optimization_barrier((mirror, pack2))
    pair = jnp.concatenate([shard, mirror], axis=0)
    slots = gather(pair, ("x", "y"), 16)
    fans = [swap(pack2, d) for d in (2, 4, 6)]
    pack8 = jnp.concatenate([pack2] + fans, axis=0)


    queries = project_queries(place, pack2, *fans, swap(pack8, 1))
    keep, send = attend(place, *queries, slots)
    merged = call(pair_kernel, shaped((8, HEADS + 1, TOK, 128)), 2, "pair")(place, keep, swap(send, 1))
    spread = lax.all_to_all(merged, ZL, 0, 0, tiled=True)
    return call(final_kernel, shaped((TOK, HEADS * VALUE)), 1, "final")(place, spread)


def solution(mesh):
    fine = Mesh(mesh.devices.reshape(2, 4, 2, 4, 4, 2), ("zq", "zr", "co", "x", "y", "zh"))
    head = ("x", "y", "zh")
    return jax.shard_map(
        per_device,
        mesh=fine,
        in_specs=(P(CTX, head), P(CTX + head, None), P(head, None, CTX), P(head, None, CTX), P()),
        out_specs=P(CTX, head),
        check_vma=False,
    )
```

```python
import math

import jax
import jax.numpy as jnp
from jax import lax
from jax.experimental import pallas as pl
from jax.experimental.pallas import tpu as pltpu
from jax.sharding import Mesh
from jax.sharding import PartitionSpec as P

PLAIN = 128
ROT = 64
LATENT = 512
VALUE = 128
HEADS = 4
WIDE = LATENT + 2 * ROT
TOK = 16
ROWS = 256
NEG = -1e30
LOG2_SCALE = (PLAIN + ROT) ** (-0.5) * math.log2(math.e)
SLOTS = 1024
MIB = 1024 * 1024

ZL = ("zq", "zr")
CTX = ("zq", "zr", "co")
f32 = jnp.float32
bf16 = jnp.bfloat16


def vmem():
    return pl.BlockSpec(memory_space=pltpu.VMEM)


def call(kernel, shape, n_in, name, scratch=(), room=8):
    return pl.pallas_call(
        kernel,
        out_shape=shape,
        in_specs=[pl.BlockSpec(memory_space=pltpu.SMEM)] + [vmem()] * n_in,
        out_specs=jax.tree.map(lambda _: vmem(), shape),
        scratch_shapes=list(scratch),
        compiler_params=pltpu.CompilerParams(vmem_limit_bytes=room * MIB),
        cost_estimate=pl.CostEstimate(flops=1, transcendentals=0, bytes_accessed=1),
        name=name,
    )


def shaped(shape, dtype=bf16):
    return jax.ShapeDtypeStruct(shape, dtype)


def prepare_kernel(queries_hbm, cache_hbm, wk_hbm, wv_hbm, shard, pack, queries, cache, sems):
    copies = [
        pltpu.make_async_copy(src, dst, sems.at[i])
        for i, (src, dst) in enumerate(
            (
                (cache_hbm, cache),
                (queries_hbm, queries),
                (wk_hbm, pack.at[0, 96:224, :]),
                (wv_hbm, pack.at[0, 224:352, :]),
            )
        )
    ]
    for c in copies:
        c.start()
    copies[0].wait()
    shard[0, :64, :] = cache[:, :LATENT]
    rot = cache[:, LATENT:]
    pairs = jnp.concatenate([rot[:32], rot[32:]], axis=1)
    for k in range(4):
        shard[0, 64:72, 128 * k : 128 * (k + 1)] = pairs[8 * k : 8 * (k + 1)]
    copies[1].wait()
    for k in range(6):
        pack[0, TOK * k : TOK * (k + 1), :] = queries[:, 128 * k : 128 * (k + 1)]
    copies[2].wait()
    copies[3].wait()


def prepare(queries, cache, wk, wv):
    return pl.pallas_call(
        prepare_kernel,
        out_shape=(shaped((1, 72, LATENT)), shaped((1, 352, 128))),
        in_specs=[pl.BlockSpec(memory_space=pltpu.HBM)] * 4,
        out_specs=(vmem(), vmem()),
        scratch_shapes=[
            pltpu.VMEM(queries.shape, bf16),
            pltpu.VMEM(cache.shape, bf16),
            pltpu.SemaphoreType.DMA((4,)),
        ],
        compiler_params=pltpu.CompilerParams(vmem_limit_bytes=4 * MIB),
        name="prepare",
    )(*(pltpu.with_memory_space_constraint(v, pltpu.HBM) for v in (queries, cache, wk, wv)))


FLIPS = ((0, 8), (2, 10), (4, 12), (6, 14), (1, 9, 3, 11, 5, 13, 7, 15))
STARTS = (0, 2, 4, 6, 8)


def query_loads(inputs, tiles, sems):
    return [
        pltpu.make_async_copy(ref, tiles.at[at : at + len(f)], sems.at[n])
        for n, (ref, at, f) in enumerate(zip(inputs, STARTS, FLIPS))
    ]


def project_queries(me, loads, tiles, pieces, panel, lats, rots, values):
    for c, at, flip in zip(loads, STARTS, FLIPS):
        c.wait()
        for i, d in enumerate(flip):
            src = lax.bitwise_xor(me, d)
            for k in range(6):
                pieces[k, src] = tiles[at + i, TOK * k : TOK * (k + 1), :]
            for h in range(HEADS):
                panel[h, src] = tiles[at + i, 96 + 32 * h : 128 + 32 * h, :]
                values[h, src] = tiles[at + i, 224 + 32 * h : 256 + 32 * h, :]
    zero = jnp.zeros((ROWS, ROT), bf16)
    for h in range(HEADS):
        k = (h // 2) * 3
        tile = [pieces[k + n].reshape(ROWS, 128) for n in range(3)]
        if h % 2 == 0:
            plain, rot = tile[0], tile[1][:, :ROT]
        else:
            plain = jnp.concatenate([tile[1][:, ROT:], tile[2][:, :ROT]], axis=1)
            rot = tile[2][:, ROT:]
        rots[0, h] = jnp.concatenate([rot, zero], axis=1)
        rots[1, h] = jnp.concatenate([zero, rot], axis=1)
        lats[h] = lax.dot_general(
            plain,
            panel[h].reshape(LATENT, PLAIN),
            (((1,), (1,)), ((), ())),
            preferred_element_type=f32,
        ).astype(bf16)


def split3(x):
    hi = x.astype(bf16)
    r = x - hi.astype(f32)
    mid = r.astype(bf16)
    lo = (r - mid.astype(f32)).astype(bf16)
    return hi, mid, lo


def pack_lse(columns, shape):
    lane = lax.broadcasted_iota(jnp.int32, shape, len(shape) - 1)
    tile = jnp.zeros(shape, f32)
    for h, column in enumerate(columns):
        for p, part in enumerate(split3(column)):
            tile = jnp.where(lane == 3 * h + p, part.astype(f32), tile)
    return tile.astype(bf16)


def lse_column(tile, h):
    t = tile.astype(f32)
    k = 3 * h
    return t[..., k : k + 1] + t[..., k + 1 : k + 2] + t[..., k + 2 : k + 3]


def attention_kernel(place, p0, p1, p2, p3, p4, chunk, keep, send, keys, turns, parts, *scratch):
    me, zh, prior = place[0], place[1], place[2]
    zl, co = lax.shift_right_logical(me, 1), lax.bitwise_and(me, 1)
    tiles, pieces, panel, lats, rots, values, sems = scratch
    loads = query_loads((p0, p1, p2, p3, p4), tiles, sems)
    for c in loads:
        c.start()
    for half in range(2):
        keys[half] = chunk[:, 32 * half : 32 * half + 32, :].reshape(SLOTS, LATENT)
    for g in range(32):
        for k in range(4):
            at = 32 * g + 8 * k
            turns[at : at + 8] = chunk[g, 64:72, 128 * k : 128 * (k + 1)]

    n = lax.broadcasted_iota(jnp.int32, (1, SLOTS), 1)
    near = ((zl * 2 + co) * 32 + zh) * 64
    far = (((7 - zl) * 2 + co) * 32 + 1 - zh) * 64
    slot = lax.shift_right_logical(n, 6) * 128 + lax.bitwise_and(n, 31)
    slot = slot + jnp.where(lax.bitwise_and(n, 32) == 0, near, far)
    project_queries(me, loads, tiles, pieces, panel, lats, rots, values)
    limit = prior + lax.bitwise_and(lax.broadcasted_iota(jnp.int32, (4 * ROWS, 1), 0), ROWS - 1)
    blocks = [(half, cut) for half in range(2) for cut in range(0, SLOTS, 512)]
    lses = []
    for first in range(0, HEADS, 4):
        group = range(first, first + 4)
        scores = []
        for half, cut in blocks:
            q = jnp.concatenate(
                [
                    lats[first : first + 4].reshape(4 * ROWS, LATENT),
                    rots[half, first : first + 4].reshape(4 * ROWS, 2 * ROT),
                ],
                axis=1,
            )
            span = slice(cut, cut + 512)
            s = lax.dot_general(
                q,
                jnp.concatenate([keys[half, span], turns[span]], axis=1),
                (((1,), (1,)), ((), ())),
                preferred_element_type=f32,
            )
            scores.append(jnp.where(slot[:, span] + 32 * half <= limit, s * LOG2_SCALE, NEG))
        peak = scores[0]
        for s in scores[1:]:
            peak = jnp.maximum(peak, s)
        peak = peak.max(axis=1, keepdims=True)
        total = jnp.zeros((4 * ROWS, 1), f32)
        acc = jnp.zeros((4 * ROWS, LATENT), f32)
        for s, (half, cut) in zip(scores, blocks):
            p = jnp.exp2(s - peak)
            total = total + p.sum(axis=1, keepdims=True)
            acc = acc + jnp.dot(p.astype(bf16), keys[half, cut : cut + 512], preferred_element_type=f32)
        latent = (acc / total).astype(bf16)
        lse = peak + jnp.log2(total)
        for i, h in enumerate(group):
            rows = slice(i * ROWS, (i + 1) * ROWS)
            o = jnp.dot(latent[rows], values[h].reshape(LATENT, VALUE), preferred_element_type=f32).astype(bf16)
            for g in range(16):
                parts[g, h] = o[TOK * g : TOK * (g + 1)]
            lses.append(lse[rows])
    tile = pack_lse(lses, (ROWS, 128))
    for g in range(16):
        parts[g, HEADS] = tile[TOK * g : TOK * (g + 1)]
    for g in range(8):
        keep[g] = parts[g * 2 + co]
        send[g] = parts[g * 2 + 1 - co]


def attend(place, slots, *pieces):
    hbm = pl.BlockSpec(memory_space=pltpu.HBM)
    return pl.pallas_call(
        attention_kernel,
        out_shape=(shaped((8, HEADS + 1, TOK, 128)),) * 2,
        in_specs=[pl.BlockSpec(memory_space=pltpu.SMEM)] + [hbm] * 5 + [vmem()],
        out_specs=(vmem(), vmem()),
        scratch_shapes=[
            pltpu.VMEM((2, SLOTS, LATENT), bf16),
            pltpu.VMEM((SLOTS, 2 * ROT), bf16),
            pltpu.VMEM((16, HEADS + 1, TOK, 128), bf16),
            pltpu.VMEM((16, 352, 128), bf16),
            pltpu.VMEM((6, 16, TOK, 128), bf16),
            pltpu.VMEM((HEADS, 16, 32, 128), bf16),
            pltpu.VMEM((HEADS, ROWS, LATENT), bf16),
            pltpu.VMEM((2, HEADS, ROWS, 2 * ROT), bf16),
            pltpu.VMEM((HEADS, 16, 32, 128), bf16),
            pltpu.SemaphoreType.DMA((5,)),
        ],
        compiler_params=pltpu.CompilerParams(vmem_limit_bytes=32 * MIB),
        name="attention",
    )(place, *(pltpu.with_memory_space_constraint(p, pltpu.HBM) for p in pieces), slots)


def merge_heads(blocks):
    tile = blocks[HEADS]
    values, lses = [], []
    for h in range(HEADS):
        column = lse_column(tile, h)
        top = column.max(axis=0)
        w = jnp.exp2(column - top)
        total = w.sum(axis=0)
        values.append((blocks[h].astype(f32) * w).sum(axis=0) / total)
        lses.append(top + jnp.log2(total))
    return values, lses


def pair_kernel(place, a, b, out):
    rows = 8 * TOK
    blocks = [
        jnp.concatenate([r[:, h].reshape(1, rows, 128) for r in (a, b)], axis=0)
        for h in range(HEADS + 1)
    ]
    values, lses = merge_heads(blocks)
    for h in range(HEADS):
        out[:, h] = values[h].astype(bf16).reshape(8, TOK, 128)
    out[:, HEADS] = pack_lse(lses, (rows, 128)).reshape(8, TOK, 128)


def final_kernel(place, x, out):
    values, _ = merge_heads([x[:, h] for h in range(HEADS + 1)])
    for h in range(HEADS):
        out[:, h * VALUE : (h + 1) * VALUE] = values[h].astype(bf16)


def swap(x, d):
    return lax.ppermute(x, CTX, [(i, i ^ d) for i in range(16)])


def gather(x, axes, n):
    copies = jnp.broadcast_to(x[None], (n, *x.shape)).reshape(n * x.shape[0], *x.shape[1:])
    return lax.all_to_all(copies, axes, 0, 0, tiled=True)


def per_device(queries, cache, key_up_weight, value_up_weight, prior_len):
    me, zh = lax.axis_index(CTX), lax.axis_index("zh")
    place = jnp.concatenate([jnp.stack([me, zh]).astype(jnp.int32), prior_len])

    shard, pack = prepare(
        queries,
        cache,
        key_up_weight.transpose(0, 2, 1).reshape(128, 128),
        value_up_weight.transpose(0, 2, 1).reshape(128, 128),
    )

    mirror = lax.ppermute(shard, ("zq", "zr", "zh"), [(i, 15 - i) for i in range(16)])
    mirror, pack = lax.optimization_barrier((mirror, pack))
    pair = jnp.concatenate([shard, mirror], axis=0)
    slots = gather(pair, ("x", "y"), 16)
    pack2 = jnp.concatenate([pack, swap(pack, 8)], axis=0)
    fans = [swap(pack2, d) for d in (2, 4, 6)]
    pack8 = jnp.concatenate([pack2] + fans, axis=0)

    keep, send = attend(place, slots, pack2, *fans, swap(pack8, 1))
    merged = call(pair_kernel, shaped((8, HEADS + 1, TOK, 128)), 2, "pair")(place, keep, swap(send, 1))
    spread = lax.all_to_all(merged, ZL, 0, 0, tiled=True)
    return call(final_kernel, shaped((TOK, HEADS * VALUE)), 1, "final")(place, spread)


def solution(mesh):
    fine = Mesh(mesh.devices.reshape(2, 4, 2, 4, 4, 2), ("zq", "zr", "co", "x", "y", "zh"))
    head = ("x", "y", "zh")
    return jax.shard_map(
        per_device,
        mesh=fine,
        in_specs=(P(CTX, head), P(CTX + head, None), P(head, None, CTX), P(head, None, CTX), P()),
        out_specs=P(CTX, head),
        check_vma=False,
    )
```

```python
import math

import jax
import jax.numpy as jnp
from jax import lax
from jax.experimental import pallas as pl
from jax.experimental.pallas import tpu as pltpu
from jax.sharding import Mesh
from jax.sharding import PartitionSpec as P

PLAIN = 128
ROT = 64
LATENT = 512
VALUE = 128
HEADS = 4
WIDE = LATENT + 2 * ROT
TOK = 16
ROWS = 256
NEG = -1e30
LOG2_SCALE = (PLAIN + ROT) ** (-0.5) * math.log2(math.e)
SLOTS = 1024
MIB = 1024 * 1024

ZL = ("zq", "zr")
CTX = ("zq", "zr", "co")
f32 = jnp.float32
bf16 = jnp.bfloat16


def vmem():
    return pl.BlockSpec(memory_space=pltpu.VMEM)


def call(kernel, shape, n_in, name, scratch=(), room=8):
    return pl.pallas_call(
        kernel,
        out_shape=shape,
        in_specs=[pl.BlockSpec(memory_space=pltpu.SMEM)] + [vmem()] * n_in,
        out_specs=jax.tree.map(lambda _: vmem(), shape),
        scratch_shapes=list(scratch),
        compiler_params=pltpu.CompilerParams(vmem_limit_bytes=room * MIB),
        cost_estimate=pl.CostEstimate(flops=1, transcendentals=0, bytes_accessed=1),
        name=name,
    )


def shaped(shape, dtype=bf16):
    return jax.ShapeDtypeStruct(shape, dtype)


def prepare_kernel(queries_hbm, cache_hbm, wk_hbm, wv_hbm, shard, pack, queries, cache, sems):
    copies = [
        pltpu.make_async_copy(src, dst, sems.at[i])
        for i, (src, dst) in enumerate(
            (
                (cache_hbm, cache),
                (queries_hbm, queries),
                (wk_hbm, pack.at[0, 96:224, :]),
                (wv_hbm, pack.at[0, 224:352, :]),
            )
        )
    ]
    for c in copies:
        c.start()
    copies[0].wait()
    shard[0, :64, :] = cache[:, :LATENT]
    rot = cache[:, LATENT:]
    pairs = jnp.concatenate([rot[:32], rot[32:]], axis=1)
    for k in range(4):
        shard[0, 64:72, 128 * k : 128 * (k + 1)] = pairs[8 * k : 8 * (k + 1)]
    copies[1].wait()
    for k in range(6):
        pack[0, TOK * k : TOK * (k + 1), :] = queries[:, 128 * k : 128 * (k + 1)]
    copies[2].wait()
    copies[3].wait()


def prepare(queries, cache, wk, wv):
    return pl.pallas_call(
        prepare_kernel,
        out_shape=(shaped((1, 72, LATENT)), shaped((1, 352, 128))),
        in_specs=[pl.BlockSpec(memory_space=pltpu.HBM)] * 4,
        out_specs=(vmem(), vmem()),
        scratch_shapes=[
            pltpu.VMEM(queries.shape, bf16),
            pltpu.VMEM(cache.shape, bf16),
            pltpu.SemaphoreType.DMA((4,)),
        ],
        compiler_params=pltpu.CompilerParams(vmem_limit_bytes=4 * MIB),
        name="prepare",
    )(*(pltpu.with_memory_space_constraint(v, pltpu.HBM) for v in (queries, cache, wk, wv)))


FLIPS = ((0, 8), (2, 10), (4, 12), (6, 14), (1, 9, 3, 11, 5, 13, 7, 15))
STARTS = (0, 2, 4, 6, 8)


def query_loads(inputs, tiles, sems):
    return [
        pltpu.make_async_copy(ref, tiles.at[at : at + len(f)], sems.at[n])
        for n, (ref, at, f) in enumerate(zip(inputs, STARTS, FLIPS))
    ]


def project_queries(me, loads, tiles, pieces, panel, lats, rots, values):
    for c, at, flip in zip(loads, STARTS, FLIPS):
        c.wait()
        for i, d in enumerate(flip):
            src = lax.bitwise_xor(me, d)
            for k in range(6):
                pieces[k, src] = tiles[at + i, TOK * k : TOK * (k + 1), :]
            for h in range(HEADS):
                panel[h, src] = tiles[at + i, 96 + 32 * h : 128 + 32 * h, :]
                values[h, src] = tiles[at + i, 224 + 32 * h : 256 + 32 * h, :]
    zero = jnp.zeros((ROWS, ROT), bf16)
    for h in range(HEADS):
        k = (h // 2) * 3
        tile = [pieces[k + n].reshape(ROWS, 128) for n in range(3)]
        if h % 2 == 0:
            plain, rot = tile[0], tile[1][:, :ROT]
        else:
            plain = jnp.concatenate([tile[1][:, ROT:], tile[2][:, :ROT]], axis=1)
            rot = tile[2][:, ROT:]
        rots[0, h] = jnp.concatenate([rot, zero], axis=1)
        rots[1, h] = jnp.concatenate([zero, rot], axis=1)
        lats[h] = lax.dot_general(
            plain,
            panel[h].reshape(LATENT, PLAIN),
            (((1,), (1,)), ((), ())),
            preferred_element_type=f32,
        ).astype(bf16)


def split3(x):
    hi = x.astype(bf16)
    r = x - hi.astype(f32)
    mid = r.astype(bf16)
    lo = (r - mid.astype(f32)).astype(bf16)
    return hi, mid, lo


def pack_lse(columns, shape):
    lane = lax.broadcasted_iota(jnp.int32, shape, len(shape) - 1)
    tile = jnp.zeros(shape, f32)
    for h, column in enumerate(columns):
        for p, part in enumerate(split3(column)):
            tile = jnp.where(lane == 3 * h + p, part.astype(f32), tile)
    return tile.astype(bf16)


def lse_column(tile, h):
    t = tile.astype(f32)
    k = 3 * h
    return t[..., k : k + 1] + t[..., k + 1 : k + 2] + t[..., k + 2 : k + 3]


def attention_kernel(place, p0, p1, p2, p3, p4, chunk, keep, send, keys, turns, parts, *scratch):
    me, zh, prior = place[0], place[1], place[2]
    zl, co = lax.shift_right_logical(me, 1), lax.bitwise_and(me, 1)
    tiles, pieces, panel, lats, rots, values, sems = scratch
    loads = query_loads((p0, p1, p2, p3, p4), tiles, sems)
    for c in loads:
        c.start()
    for half in range(2):
        keys[half] = chunk[:, 32 * half : 32 * half + 32, :].reshape(SLOTS, LATENT)
    for g in range(32):
        for k in range(4):
            at = 32 * g + 8 * k
            turns[at : at + 8] = chunk[g, 64:72, 128 * k : 128 * (k + 1)]

    n = lax.broadcasted_iota(jnp.int32, (1, SLOTS), 1)
    near = ((zl * 2 + co) * 32 + zh) * 64
    far = (((7 - zl) * 2 + co) * 32 + 1 - zh) * 64
    slot = lax.shift_right_logical(n, 6) * 128 + lax.bitwise_and(n, 31)
    slot = slot + jnp.where(lax.bitwise_and(n, 32) == 0, near, far)
    project_queries(me, loads, tiles, pieces, panel, lats, rots, values)
    limit = prior + lax.bitwise_and(lax.broadcasted_iota(jnp.int32, (4 * ROWS, 1), 0), ROWS - 1)
    blocks = [(half, cut) for half in range(2) for cut in range(0, SLOTS, 512)]
    lses = []
    for first in range(0, HEADS, 4):
        group = range(first, first + 4)
        scores = []
        for half, cut in blocks:
            q = jnp.concatenate(
                [
                    lats[first : first + 4].reshape(4 * ROWS, LATENT),
                    rots[half, first : first + 4].reshape(4 * ROWS, 2 * ROT),
                ],
                axis=1,
            )
            span = slice(cut, cut + 512)
            s = lax.dot_general(
                q,
                jnp.concatenate([keys[half, span], turns[span]], axis=1),
                (((1,), (1,)), ((), ())),
                preferred_element_type=f32,
            )
            scores.append(jnp.where(slot[:, span] + 32 * half <= limit, s * LOG2_SCALE, NEG))
        peak = scores[0]
        for s in scores[1:]:
            peak = jnp.maximum(peak, s)
        peak = peak.max(axis=1, keepdims=True)
        total = jnp.zeros((4 * ROWS, 1), f32)
        acc = jnp.zeros((4 * ROWS, LATENT), f32)
        for s, (half, cut) in zip(scores, blocks):
            p = jnp.exp2(s - peak)
            total = total + p.sum(axis=1, keepdims=True)
            acc = acc + jnp.dot(p.astype(bf16), keys[half, cut : cut + 512], preferred_element_type=f32)
        latent = (acc / total).astype(bf16)
        lse = peak + jnp.log2(total)
        for i, h in enumerate(group):
            rows = slice(i * ROWS, (i + 1) * ROWS)
            o = jnp.dot(latent[rows], values[h].reshape(LATENT, VALUE), preferred_element_type=f32).astype(bf16)
            for g in range(16):
                parts[g, h] = o[TOK * g : TOK * (g + 1)]
            lses.append(lse[rows])
    tile = pack_lse(lses, (ROWS, 128))
    for g in range(16):
        parts[g, HEADS] = tile[TOK * g : TOK * (g + 1)]
    for g in range(8):
        keep[g] = parts[g * 2 + co]
        send[g] = parts[g * 2 + 1 - co]


def attend(place, slots, *pieces):
    hbm = pl.BlockSpec(memory_space=pltpu.HBM)
    return pl.pallas_call(
        attention_kernel,
        out_shape=(shaped((8, HEADS + 1, TOK, 128)),) * 2,
        in_specs=[pl.BlockSpec(memory_space=pltpu.SMEM)] + [hbm] * 5 + [vmem()],
        out_specs=(vmem(), vmem()),
        scratch_shapes=[
            pltpu.VMEM((2, SLOTS, LATENT), bf16),
            pltpu.VMEM((SLOTS, 2 * ROT), bf16),
            pltpu.VMEM((16, HEADS + 1, TOK, 128), bf16),
            pltpu.VMEM((16, 352, 128), bf16),
            pltpu.VMEM((6, 16, TOK, 128), bf16),
            pltpu.VMEM((HEADS, 16, 32, 128), bf16),
            pltpu.VMEM((HEADS, ROWS, LATENT), bf16),
            pltpu.VMEM((2, HEADS, ROWS, 2 * ROT), bf16),
            pltpu.VMEM((HEADS, 16, 32, 128), bf16),
            pltpu.SemaphoreType.DMA((5,)),
        ],
        compiler_params=pltpu.CompilerParams(vmem_limit_bytes=32 * MIB),
        name="attention",
    )(place, *(pltpu.with_memory_space_constraint(p, pltpu.HBM) for p in pieces), slots)


def merge_heads(blocks):
    tile = blocks[HEADS]
    values, lses = [], []
    for h in range(HEADS):
        column = lse_column(tile, h)
        top = column.max(axis=0)
        w = jnp.exp2(column - top)
        total = w.sum(axis=0)
        values.append((blocks[h].astype(f32) * w).sum(axis=0) / total)
        lses.append(top + jnp.log2(total))
    return values, lses


def pair_kernel(place, a, b, out):
    rows = 8 * TOK
    blocks = [
        jnp.concatenate([r[:, h].reshape(1, rows, 128) for r in (a, b)], axis=0)
        for h in range(HEADS + 1)
    ]
    values, lses = merge_heads(blocks)
    for h in range(HEADS):
        out[:, h] = values[h].astype(bf16).reshape(8, TOK, 128)
    out[:, HEADS] = pack_lse(lses, (rows, 128)).reshape(8, TOK, 128)


def final_kernel(place, x, out):
    values, _ = merge_heads([x[:, h] for h in range(HEADS + 1)])
    for h in range(HEADS):
        out[:, h * VALUE : (h + 1) * VALUE] = values[h].astype(bf16)


def swap(x, d):
    return lax.ppermute(x, CTX, [(i, i ^ d) for i in range(16)])


def gather(x, axes, n):
    copies = jnp.broadcast_to(x[None], (n, *x.shape)).reshape(n * x.shape[0], *x.shape[1:])
    return lax.all_to_all(copies, axes, 0, 0, tiled=True)


def per_device(queries, cache, key_up_weight, value_up_weight, prior_len):
    me, zh = lax.axis_index(CTX), lax.axis_index("zh")
    place = jnp.concatenate([jnp.stack([me, zh]).astype(jnp.int32), prior_len])

    shard, pack = prepare(
        queries,
        cache,
        key_up_weight.transpose(0, 2, 1).reshape(128, 128),
        value_up_weight.transpose(0, 2, 1).reshape(128, 128),
    )

    mirror = lax.ppermute(shard, ("zq", "zr", "zh"), [(i, 15 - i) for i in range(16)])
    got = swap(pack, 8)
    pair = jnp.concatenate([shard, mirror], axis=0)
    copies = jnp.broadcast_to(pair[None], (16, 2, 72, LATENT)).reshape(32, 72, LATENT)
    pack2 = jnp.concatenate([pack, got], axis=0)
    copies, pack2 = lax.optimization_barrier((copies, pack2))
    slots = lax.all_to_all(copies, ("x", "y"), 0, 0, tiled=True)
    fans = [swap(pack2, d) for d in (2, 4, 6)]
    pack8 = jnp.concatenate([pack2] + fans, axis=0)

    keep, send = attend(place, slots, pack2, *fans, swap(pack8, 1))
    merged = call(pair_kernel, shaped((8, HEADS + 1, TOK, 128)), 2, "pair")(place, keep, swap(send, 1))
    spread = lax.all_to_all(merged, ZL, 0, 0, tiled=True)
    return call(final_kernel, shaped((TOK, HEADS * VALUE)), 1, "final")(place, spread)


def solution(mesh):
    fine = Mesh(mesh.devices.reshape(2, 4, 2, 4, 4, 2), ("zq", "zr", "co", "x", "y", "zh"))
    head = ("x", "y", "zh")
    return jax.shard_map(
        per_device,
        mesh=fine,
        in_specs=(P(CTX, head), P(CTX + head, None), P(head, None, CTX), P(head, None, CTX), P()),
        out_specs=P(CTX, head),
        check_vma=False,
    )
```

```python
import math

import jax
import jax.numpy as jnp
from jax import lax
from jax.experimental import pallas as pl
from jax.experimental.pallas import tpu as pltpu
from jax.sharding import Mesh
from jax.sharding import PartitionSpec as P

PLAIN = 128
ROT = 64
LATENT = 512
VALUE = 128
HEADS = 4
WIDE = LATENT + 2 * ROT
TOK = 16
ROWS = 256
NEG = -1e30
LOG2_SCALE = (PLAIN + ROT) ** (-0.5) * math.log2(math.e)
SLOTS = 1024
MIB = 1024 * 1024

ZL = ("zq", "zr")
CTX = ("zq", "zr", "co")
f32 = jnp.float32
bf16 = jnp.bfloat16


def vmem():
    return pl.BlockSpec(memory_space=pltpu.VMEM)


def call(kernel, shape, n_in, name):
    return pl.pallas_call(
        kernel,
        out_shape=shape,
        in_specs=[vmem()] * n_in,
        out_specs=vmem(),
        compiler_params=pltpu.CompilerParams(vmem_limit_bytes=8 * MIB),
        name=name,
    )


def shaped(shape, dtype=bf16):
    return jax.ShapeDtypeStruct(shape, dtype)


def prepare_kernel(queries_hbm, cache_hbm, wk_hbm, wv_hbm, shard, pack, queries, cache, sems):
    copies = [
        pltpu.make_async_copy(src, dst, sems.at[i])
        for i, (src, dst) in enumerate(
            (
                (cache_hbm, cache),
                (queries_hbm, queries),
                (wk_hbm, pack.at[0, 96:224, :]),
                (wv_hbm, pack.at[0, 224:352, :]),
            )
        )
    ]
    for c in copies:
        c.start()
    copies[0].wait()
    shard[0, :64, :] = cache[:, :LATENT]
    rot = cache[:, LATENT:]
    pairs = jnp.concatenate([rot[:32], rot[32:]], axis=1)
    for k in range(4):
        shard[0, 64:72, 128 * k : 128 * (k + 1)] = pairs[8 * k : 8 * (k + 1)]
    copies[1].wait()
    for k in range(6):
        pack[0, TOK * k : TOK * (k + 1), :] = queries[:, 128 * k : 128 * (k + 1)]
    copies[2].wait()
    copies[3].wait()


def prepare(queries, cache, wk, wv):
    return pl.pallas_call(
        prepare_kernel,
        out_shape=(shaped((1, 72, LATENT)), shaped((1, 352, 128))),
        in_specs=[pl.BlockSpec(memory_space=pltpu.HBM)] * 4,
        out_specs=(vmem(), vmem()),
        scratch_shapes=[
            pltpu.VMEM(queries.shape, bf16),
            pltpu.VMEM(cache.shape, bf16),
            pltpu.SemaphoreType.DMA((4,)),
        ],
        compiler_params=pltpu.CompilerParams(vmem_limit_bytes=4 * MIB),
        name="prepare",
    )(*(pltpu.with_memory_space_constraint(v, pltpu.HBM) for v in (queries, cache, wk, wv)))


FLIPS = ((0, 8), (2, 10), (4, 12), (6, 14), (1, 9, 3, 11, 5, 13, 7, 15))
STARTS = (0, 2, 4, 6, 8)


def query_loads(inputs, tiles, sems):
    return [
        pltpu.make_async_copy(ref, tiles.at[at : at + len(f)], sems.at[n])
        for n, (ref, at, f) in enumerate(zip(inputs, STARTS, FLIPS))
    ]


def project_queries(me, loads, tiles, pieces, panel, lats, rots, values):
    for c, at, flip in zip(loads, STARTS, FLIPS):
        c.wait()
        for i, d in enumerate(flip):
            src = lax.bitwise_xor(me, d)
            for k in range(6):
                pieces[k, src] = tiles[at + i, TOK * k : TOK * (k + 1), :]
            for h in range(HEADS):
                panel[h, src] = tiles[at + i, 96 + 32 * h : 128 + 32 * h, :]
                values[h, src] = tiles[at + i, 224 + 32 * h : 256 + 32 * h, :]
    zero = jnp.zeros((ROWS, ROT), bf16)
    for h in range(HEADS):
        k = (h // 2) * 3
        tile = [pieces[k + n].reshape(ROWS, 128) for n in range(3)]
        if h % 2 == 0:
            plain, rot = tile[0], tile[1][:, :ROT]
        else:
            plain = jnp.concatenate([tile[1][:, ROT:], tile[2][:, :ROT]], axis=1)
            rot = tile[2][:, ROT:]
        rots[0, h] = jnp.concatenate([rot, zero], axis=1)
        rots[1, h] = jnp.concatenate([zero, rot], axis=1)
        lats[h] = lax.dot_general(
            plain,
            panel[h].reshape(LATENT, PLAIN),
            (((1,), (1,)), ((), ())),
            preferred_element_type=f32,
        ).astype(bf16)


def split3(x):
    hi = x.astype(bf16)
    r = x - hi.astype(f32)
    mid = r.astype(bf16)
    lo = (r - mid.astype(f32)).astype(bf16)
    return hi, mid, lo


def pack_lse(columns, shape):
    lane = lax.broadcasted_iota(jnp.int32, shape, len(shape) - 1)
    tile = jnp.zeros(shape, f32)
    for h, column in enumerate(columns):
        for p, part in enumerate(split3(column)):
            tile = jnp.where(lane == 3 * h + p, part.astype(f32), tile)
    return tile.astype(bf16)


def lse_column(tile, h):
    t = tile.astype(f32)
    k = 3 * h
    return t[..., k : k + 1] + t[..., k + 1 : k + 2] + t[..., k + 2 : k + 3]


def attention_kernel(place, token, p0, p1, p2, p3, p4, chunk, keep, send, keys, turns, parts, *scratch):
    me, zh, prior = place[0], place[1], place[2]
    zl, co = lax.shift_right_logical(me, 1), lax.bitwise_and(me, 1)
    tiles, pieces, panel, lats, rots, values, sems = scratch
    loads = query_loads((p0, p1, p2, p3, p4), tiles, sems)
    for c in loads:
        c.start()
    for half in range(2):
        keys[half] = chunk[:, 32 * half : 32 * half + 32, :].reshape(SLOTS, LATENT)
    for g in range(32):
        for k in range(4):
            at = 32 * g + 8 * k
            turns[at : at + 8] = chunk[g, 64:72, 128 * k : 128 * (k + 1)]

    n = lax.broadcasted_iota(jnp.int32, (1, SLOTS), 1)
    near = ((zl * 2 + co) * 32 + zh) * 64
    far = (((7 - zl) * 2 + co) * 32 + 1 - zh) * 64
    slot = lax.shift_right_logical(n, 6) * 128 + lax.bitwise_and(n, 31)
    slot = slot + jnp.where(lax.bitwise_and(n, 32) == 0, near, far)
    project_queries(me, loads, tiles, pieces, panel, lats, rots, values)
    limit = prior + lax.bitwise_and(lax.broadcasted_iota(jnp.int32, (4 * ROWS, 1), 0), ROWS - 1)
    blocks = [(half, cut) for half in range(2) for cut in range(0, SLOTS, 512)]
    lses = []
    for first in range(0, HEADS, 4):
        group = range(first, first + 4)
        scores = []
        for half, cut in blocks:
            q = jnp.concatenate(
                [
                    lats[first : first + 4].reshape(4 * ROWS, LATENT),
                    rots[half, first : first + 4].reshape(4 * ROWS, 2 * ROT),
                ],
                axis=1,
            )
            span = slice(cut, cut + 512)
            s = lax.dot_general(
                q,
                jnp.concatenate([keys[half, span], turns[span]], axis=1),
                (((1,), (1,)), ((), ())),
                preferred_element_type=f32,
            )
            scores.append(jnp.where(slot[:, span] + 32 * half <= limit, s * LOG2_SCALE, NEG))
        peak = scores[0]
        for s in scores[1:]:
            peak = jnp.maximum(peak, s)
        peak = peak.max(axis=1, keepdims=True)
        total = jnp.zeros((4 * ROWS, 1), f32)
        acc = jnp.zeros((4 * ROWS, LATENT), f32)
        for s, (half, cut) in zip(scores, blocks):
            p = jnp.exp2(s - peak)
            total = total + p.sum(axis=1, keepdims=True)
            acc = acc + jnp.dot(p.astype(bf16), keys[half, cut : cut + 512], preferred_element_type=f32)
        latent = (acc / total).astype(bf16)
        lse = peak + jnp.log2(total)
        for i, h in enumerate(group):
            rows = slice(i * ROWS, (i + 1) * ROWS)
            o = jnp.dot(latent[rows], values[h].reshape(LATENT, VALUE), preferred_element_type=f32).astype(bf16)
            for g in range(16):
                parts[g, h] = o[TOK * g : TOK * (g + 1)]
            lses.append(lse[rows])
    tile = pack_lse(lses, (ROWS, 128))
    for g in range(16):
        parts[g, HEADS] = tile[TOK * g : TOK * (g + 1)]
    for g in range(8):
        keep[g] = parts[g * 2 + co]
        send[g] = parts[g * 2 + 1 - co]


def attend(place, slots, *pieces):
    hbm = pl.BlockSpec(memory_space=pltpu.HBM)
    return pl.pallas_call(
        attention_kernel,
        out_shape=(shaped((8, HEADS + 1, TOK, 128)),) * 2,
        in_specs=[pl.BlockSpec(memory_space=pltpu.SMEM)] + [hbm] * 6 + [vmem()],
        out_specs=(vmem(), vmem()),
        scratch_shapes=[
            pltpu.VMEM((2, SLOTS, LATENT), bf16),
            pltpu.VMEM((SLOTS, 2 * ROT), bf16),
            pltpu.VMEM((16, HEADS + 1, TOK, 128), bf16),
            pltpu.VMEM((16, 352, 128), bf16),
            pltpu.VMEM((6, 16, TOK, 128), bf16),
            pltpu.VMEM((HEADS, 16, 32, 128), bf16),
            pltpu.VMEM((HEADS, ROWS, LATENT), bf16),
            pltpu.VMEM((2, HEADS, ROWS, 2 * ROT), bf16),
            pltpu.VMEM((HEADS, 16, 32, 128), bf16),
            pltpu.SemaphoreType.DMA((5,)),
        ],
        compiler_params=pltpu.CompilerParams(vmem_limit_bytes=32 * MIB),
        name="attention",
    )(place, *(pltpu.with_memory_space_constraint(p, pltpu.HBM) for p in pieces), slots)


def arrival_kernel(last, out, token, sem):
    token[...] = jnp.zeros_like(token)
    copy = pltpu.make_async_copy(token, out, sem)
    copy.start()
    copy.wait()


def arrival(last):
    hbm = pl.BlockSpec(memory_space=pltpu.HBM)
    return pl.pallas_call(
        arrival_kernel,
        out_shape=pltpu.HBM((8, 128), f32),
        in_specs=[hbm],
        out_specs=hbm,
        scratch_shapes=[pltpu.VMEM((8, 128), f32), pltpu.SemaphoreType.DMA],
        cost_estimate=pl.CostEstimate(flops=11500000000, transcendentals=0, bytes_accessed=0),
        compiler_params=pltpu.CompilerParams(vmem_limit_bytes=MIB),
        name="arrival",
    )(pltpu.with_memory_space_constraint(last, pltpu.HBM))


def merge_heads(blocks):
    tile = blocks[HEADS]
    values, lses = [], []
    for h in range(HEADS):
        column = lse_column(tile, h)
        top = column.max(axis=0)
        w = jnp.exp2(column - top)
        total = w.sum(axis=0)
        values.append((blocks[h].astype(f32) * w).sum(axis=0) / total)
        lses.append(top + jnp.log2(total))
    return values, lses


def pair_kernel(a, b, out):
    rows = 8 * TOK
    blocks = [
        jnp.concatenate([r[:, h].reshape(1, rows, 128) for r in (a, b)], axis=0)
        for h in range(HEADS + 1)
    ]
    values, lses = merge_heads(blocks)
    for h in range(HEADS):
        out[:, h] = values[h].astype(bf16).reshape(8, TOK, 128)
    out[:, HEADS] = pack_lse(lses, (rows, 128)).reshape(8, TOK, 128)


def final_kernel(x, out):
    values, _ = merge_heads([x[:, h] for h in range(HEADS + 1)])
    for h in range(HEADS):
        out[:, h * VALUE : (h + 1) * VALUE] = values[h].astype(bf16)


def swap(x, d):
    return lax.ppermute(x, CTX, [(i, i ^ d) for i in range(16)])


def gather(x, axes, n):
    copies = jnp.broadcast_to(x[None], (n, *x.shape)).reshape(n * x.shape[0], *x.shape[1:])
    return lax.all_to_all(copies, axes, 0, 0, tiled=True)


def per_device(queries, cache, key_up_weight, value_up_weight, prior_len):
    me, zh = lax.axis_index(CTX), lax.axis_index("zh")
    place = jnp.concatenate([jnp.stack([me, zh]).astype(jnp.int32), prior_len])

    shard, pack = prepare(
        queries,
        cache,
        key_up_weight.transpose(0, 2, 1).reshape(128, 128),
        value_up_weight.transpose(0, 2, 1).reshape(128, 128),
    )

    mirror = lax.ppermute(shard, ("zq", "zr", "zh"), [(i, 15 - i) for i in range(16)])
    pack2 = jnp.concatenate([pack, swap(pack, 8)], axis=0)
    _, pack2 = lax.optimization_barrier((mirror, pack2))
    pair = jnp.concatenate([shard, mirror], axis=0)
    slots = gather(pair, ("x", "y"), 16)
    fans = [swap(pack2, d) for d in (2, 4, 6)]
    pack8 = jnp.concatenate([pack2] + fans, axis=0)

    last = swap(pack8, 1)
    keep, send = attend(place, slots, arrival(last), pack2, *fans, last)
    merged = call(pair_kernel, shaped((8, HEADS + 1, TOK, 128)), 2, "pair")(keep, swap(send, 1))
    spread = lax.all_to_all(merged, ZL, 0, 0, tiled=True)
    return call(final_kernel, shaped((TOK, HEADS * VALUE)), 1, "final")(spread)


def solution(mesh):
    fine = Mesh(mesh.devices.reshape(2, 4, 2, 4, 4, 2), ("zq", "zr", "co", "x", "y", "zh"))
    head = ("x", "y", "zh")
    return jax.shard_map(
        per_device,
        mesh=fine,
        in_specs=(P(CTX, head), P(CTX + head, None), P(head, None, CTX), P(head, None, CTX), P()),
        out_specs=P(CTX, head),
        check_vma=False,
    )
```

```python
import math

import jax
import jax.numpy as jnp
from jax import lax
from jax.experimental import pallas as pl
from jax.experimental.pallas import tpu as pltpu
from jax.sharding import Mesh
from jax.sharding import PartitionSpec as P

PLAIN = 128
ROT = 64
LATENT = 512
VALUE = 128
HEADS = 4
WIDE = LATENT + 2 * ROT
TOK = 16
ROWS = 256
NEG = -1e30
LOG2_SCALE = (PLAIN + ROT) ** (-0.5) * math.log2(math.e)
SLOTS = 1024
MIB = 1024 * 1024

ZL = ("zq", "zr")
CTX = ("zq", "zr", "co")
f32 = jnp.float32
bf16 = jnp.bfloat16


def vmem():
    return pl.BlockSpec(memory_space=pltpu.VMEM)


def call(kernel, shape, n_in, name):
    return pl.pallas_call(
        kernel,
        out_shape=shape,
        in_specs=[vmem()] * n_in,
        out_specs=vmem(),
        compiler_params=pltpu.CompilerParams(vmem_limit_bytes=8 * MIB),
        name=name,
    )


def shaped(shape, dtype=bf16):
    return jax.ShapeDtypeStruct(shape, dtype)


def prepare_kernel(queries_hbm, cache_hbm, wk_hbm, wv_hbm, shard, pack, queries, cache, sems):
    copies = [
        pltpu.make_async_copy(src, dst, sems.at[i])
        for i, (src, dst) in enumerate(
            (
                (cache_hbm, cache),
                (queries_hbm, queries),
                (wk_hbm, pack.at[0, 96:224, :]),
                (wv_hbm, pack.at[0, 224:352, :]),
            )
        )
    ]
    for c in copies:
        c.start()
    copies[0].wait()
    shard[0, :64, :] = cache[:, :LATENT]
    rot = cache[:, LATENT:]
    pairs = jnp.concatenate([rot[:32], rot[32:]], axis=1)
    for k in range(4):
        shard[0, 64:72, 128 * k : 128 * (k + 1)] = pairs[8 * k : 8 * (k + 1)]
    copies[1].wait()
    for k in range(6):
        pack[0, TOK * k : TOK * (k + 1), :] = queries[:, 128 * k : 128 * (k + 1)]
    copies[2].wait()
    copies[3].wait()


def prepare(queries, cache, wk, wv):
    return pl.pallas_call(
        prepare_kernel,
        out_shape=(shaped((1, 72, LATENT)), shaped((1, 352, 128))),
        in_specs=[pl.BlockSpec(memory_space=pltpu.HBM)] * 4,
        out_specs=(vmem(), vmem()),
        scratch_shapes=[
            pltpu.VMEM(queries.shape, bf16),
            pltpu.VMEM(cache.shape, bf16),
            pltpu.SemaphoreType.DMA((4,)),
        ],
        compiler_params=pltpu.CompilerParams(vmem_limit_bytes=4 * MIB),
        name="prepare",
    )(*(pltpu.with_memory_space_constraint(v, pltpu.HBM) for v in (queries, cache, wk, wv)))


FLIPS = ((0, 8), (2, 10), (4, 12), (6, 14), (1, 9, 3, 11, 5, 13, 7, 15))
STARTS = (0, 2, 4, 6, 8)


def query_loads(inputs, tiles, sems):
    return [
        pltpu.make_async_copy(ref, tiles.at[at : at + len(f)], sems.at[n])
        for n, (ref, at, f) in enumerate(zip(inputs, STARTS, FLIPS))
    ]


def project_queries(me, loads, tiles, pieces, panel, lats, rots, values):
    for c, at, flip in zip(loads, STARTS, FLIPS):
        c.wait()
        for i, d in enumerate(flip):
            src = lax.bitwise_xor(me, d)
            for k in range(6):
                pieces[k, src] = tiles[at + i, TOK * k : TOK * (k + 1), :]
            for h in range(HEADS):
                panel[h, src] = tiles[at + i, 96 + 32 * h : 128 + 32 * h, :]
                values[h, src] = tiles[at + i, 224 + 32 * h : 256 + 32 * h, :]
    zero = jnp.zeros((ROWS, ROT), bf16)
    for h in range(HEADS):
        k = (h // 2) * 3
        tile = [pieces[k + n].reshape(ROWS, 128) for n in range(3)]
        if h % 2 == 0:
            plain, rot = tile[0], tile[1][:, :ROT]
        else:
            plain = jnp.concatenate([tile[1][:, ROT:], tile[2][:, :ROT]], axis=1)
            rot = tile[2][:, ROT:]
        rots[0, h] = jnp.concatenate([rot, zero], axis=1)
        rots[1, h] = jnp.concatenate([zero, rot], axis=1)
        lats[h] = lax.dot_general(
            plain,
            panel[h].reshape(LATENT, PLAIN),
            (((1,), (1,)), ((), ())),
            preferred_element_type=f32,
        ).astype(bf16)


def split3(x):
    hi = x.astype(bf16)
    r = x - hi.astype(f32)
    mid = r.astype(bf16)
    lo = (r - mid.astype(f32)).astype(bf16)
    return hi, mid, lo


def pack_lse(columns, shape):
    lane = lax.broadcasted_iota(jnp.int32, shape, len(shape) - 1)
    tile = jnp.zeros(shape, f32)
    for h, column in enumerate(columns):
        for p, part in enumerate(split3(column)):
            tile = jnp.where(lane == 3 * h + p, part.astype(f32), tile)
    return tile.astype(bf16)


def lse_column(tile, h):
    t = tile.astype(f32)
    k = 3 * h
    return t[..., k : k + 1] + t[..., k + 1 : k + 2] + t[..., k + 2 : k + 3]


def attention_kernel(place, token, p0, p1, p2, p3, p4, chunk, keep, send, keys, turns, parts, *scratch):
    me, zh, prior = place[0], place[1], place[2]
    zl, co = lax.shift_right_logical(me, 1), lax.bitwise_and(me, 1)
    tiles, pieces, panel, lats, rots, values, sems = scratch
    loads = query_loads((p0, p1, p2, p3, p4), tiles, sems)
    for c in loads:
        c.start()
    for half in range(2):
        keys[half] = chunk[:, 32 * half : 32 * half + 32, :].reshape(SLOTS, LATENT)
    for g in range(32):
        for k in range(4):
            at = 32 * g + 8 * k
            turns[at : at + 8] = chunk[g, 64:72, 128 * k : 128 * (k + 1)]

    n = lax.broadcasted_iota(jnp.int32, (1, SLOTS), 1)
    near = ((zl * 2 + co) * 32 + zh) * 64
    far = (((7 - zl) * 2 + co) * 32 + 1 - zh) * 64
    slot = lax.shift_right_logical(n, 6) * 128 + lax.bitwise_and(n, 31)
    slot = slot + jnp.where(lax.bitwise_and(n, 32) == 0, near, far)
    project_queries(me, loads, tiles, pieces, panel, lats, rots, values)
    limit = prior + lax.bitwise_and(lax.broadcasted_iota(jnp.int32, (4 * ROWS, 1), 0), ROWS - 1)
    blocks = [(half, cut) for half in range(2) for cut in range(0, SLOTS, 512)]
    lses = []
    for first in range(0, HEADS, 4):
        group = range(first, first + 4)
        scores = []
        for half, cut in blocks:
            q = jnp.concatenate(
                [
                    lats[first : first + 4].reshape(4 * ROWS, LATENT),
                    rots[half, first : first + 4].reshape(4 * ROWS, 2 * ROT),
                ],
                axis=1,
            )
            span = slice(cut, cut + 512)
            s = lax.dot_general(
                q,
                jnp.concatenate([keys[half, span], turns[span]], axis=1),
                (((1,), (1,)), ((), ())),
                preferred_element_type=f32,
            )
            scores.append(jnp.where(slot[:, span] + 32 * half <= limit, s * LOG2_SCALE, NEG))
        peak = scores[0]
        for s in scores[1:]:
            peak = jnp.maximum(peak, s)
        peak = peak.max(axis=1, keepdims=True)
        total = jnp.zeros((4 * ROWS, 1), f32)
        acc = jnp.zeros((4 * ROWS, LATENT), f32)
        for s, (half, cut) in zip(scores, blocks):
            p = jnp.exp2(s - peak)
            total = total + p.sum(axis=1, keepdims=True)
            acc = acc + jnp.dot(p.astype(bf16), keys[half, cut : cut + 512], preferred_element_type=f32)
        latent = (acc / total).astype(bf16)
        lse = peak + jnp.log2(total)
        for i, h in enumerate(group):
            rows = slice(i * ROWS, (i + 1) * ROWS)
            o = jnp.dot(latent[rows], values[h].reshape(LATENT, VALUE), preferred_element_type=f32).astype(bf16)
            for g in range(16):
                parts[g, h] = o[TOK * g : TOK * (g + 1)]
            lses.append(lse[rows])
    tile = pack_lse(lses, (ROWS, 128))
    for g in range(16):
        parts[g, HEADS] = tile[TOK * g : TOK * (g + 1)]
    for g in range(8):
        keep[g] = parts[g * 2 + co]
        send[g] = parts[g * 2 + 1 - co]


def attend(place, slots, *pieces):
    hbm = pl.BlockSpec(memory_space=pltpu.HBM)
    return pl.pallas_call(
        attention_kernel,
        out_shape=(shaped((8, HEADS + 1, TOK, 128)),) * 2,
        in_specs=[pl.BlockSpec(memory_space=pltpu.SMEM)] + [hbm] * 6 + [vmem()],
        out_specs=(vmem(), vmem()),
        scratch_shapes=[
            pltpu.VMEM((2, SLOTS, LATENT), bf16),
            pltpu.VMEM((SLOTS, 2 * ROT), bf16),
            pltpu.VMEM((16, HEADS + 1, TOK, 128), bf16),
            pltpu.VMEM((16, 352, 128), bf16),
            pltpu.VMEM((6, 16, TOK, 128), bf16),
            pltpu.VMEM((HEADS, 16, 32, 128), bf16),
            pltpu.VMEM((HEADS, ROWS, LATENT), bf16),
            pltpu.VMEM((2, HEADS, ROWS, 2 * ROT), bf16),
            pltpu.VMEM((HEADS, 16, 32, 128), bf16),
            pltpu.SemaphoreType.DMA((5,)),
        ],
        compiler_params=pltpu.CompilerParams(vmem_limit_bytes=32 * MIB),
        name="attention",
    )(place, *(pltpu.with_memory_space_constraint(p, pltpu.HBM) for p in pieces), slots)


def arrival_kernel(last, out, token, sem):
    token[...] = jnp.zeros_like(token)
    copy = pltpu.make_async_copy(token, out, sem)
    copy.start()
    copy.wait()


def arrival(last):
    hbm = pl.BlockSpec(memory_space=pltpu.HBM)
    return pl.pallas_call(
        arrival_kernel,
        out_shape=pltpu.HBM((8, 128), f32),
        in_specs=[hbm],
        out_specs=hbm,
        scratch_shapes=[pltpu.VMEM((8, 128), f32), pltpu.SemaphoreType.DMA],
        cost_estimate=pl.CostEstimate(flops=11000000000, transcendentals=0, bytes_accessed=0),
        compiler_params=pltpu.CompilerParams(vmem_limit_bytes=MIB),
        name="arrival",
    )(pltpu.with_memory_space_constraint(last, pltpu.HBM))


def merge_heads(blocks):
    tile = blocks[HEADS]
    values, lses = [], []
    for h in range(HEADS):
        column = lse_column(tile, h)
        top = column.max(axis=0)
        w = jnp.exp2(column - top)
        total = w.sum(axis=0)
        values.append((blocks[h].astype(f32) * w).sum(axis=0) / total)
        lses.append(top + jnp.log2(total))
    return values, lses


def pair_kernel(a, b, out):
    rows = 8 * TOK
    blocks = [
        jnp.concatenate([r[:, h].reshape(1, rows, 128) for r in (a, b)], axis=0)
        for h in range(HEADS + 1)
    ]
    values, lses = merge_heads(blocks)
    for h in range(HEADS):
        out[:, h] = values[h].astype(bf16).reshape(8, TOK, 128)
    out[:, HEADS] = pack_lse(lses, (rows, 128)).reshape(8, TOK, 128)


def final_kernel(x, out):
    values, _ = merge_heads([x[:, h] for h in range(HEADS + 1)])
    for h in range(HEADS):
        out[:, h * VALUE : (h + 1) * VALUE] = values[h].astype(bf16)


def swap(x, d):
    return lax.ppermute(x, CTX, [(i, i ^ d) for i in range(16)])


def replicate(half, block, copies=None):
    hbm = pl.BlockSpec(memory_space=pltpu.HBM)

    def spread_kernel(block, *refs):
        out, sems = refs[-2:]
        writes = [
            pltpu.make_async_copy(block, out.at[n, half : half + 1], sems.at[n]) for n in range(16)
        ]
        for w in writes:
            w.start()
        for w in writes:
            w.wait()

    operands = (block,) if copies is None else (block, copies)
    return pl.pallas_call(
        spread_kernel,
        out_shape=pltpu.HBM((16, 2, 72, LATENT), bf16),
        in_specs=[vmem()] + [hbm] * (len(operands) - 1),
        out_specs=hbm,
        scratch_shapes=[pltpu.SemaphoreType.DMA((16,))],
        input_output_aliases={} if copies is None else {1: 0},
        compiler_params=pltpu.CompilerParams(vmem_limit_bytes=MIB),
        name=f"spread{half}",
    )(*operands)


def per_device(queries, cache, key_up_weight, value_up_weight, prior_len):
    me, zh = lax.axis_index(CTX), lax.axis_index("zh")
    place = jnp.concatenate([jnp.stack([me, zh]).astype(jnp.int32), prior_len])

    shard, pack = prepare(
        queries,
        cache,
        key_up_weight.transpose(0, 2, 1).reshape(128, 128),
        value_up_weight.transpose(0, 2, 1).reshape(128, 128),
    )

    mirror = lax.ppermute(shard, ("zq", "zr", "zh"), [(i, 15 - i) for i in range(16)])
    pack2 = jnp.concatenate([pack, swap(pack, 8)], axis=0)
    _, pack2 = lax.optimization_barrier((mirror, pack2))
    copies = replicate(1, mirror, replicate(0, shard))
    slots = lax.all_to_all(copies.reshape(32, 72, LATENT), ("x", "y"), 0, 0, tiled=True)
    fans = [swap(pack2, d) for d in (2, 4, 6)]
    pack8 = jnp.concatenate([pack2] + fans, axis=0)

    last = swap(pack8, 1)
    keep, send = attend(place, slots, arrival(last), pack2, *fans, last)
    merged = call(pair_kernel, shaped((8, HEADS + 1, TOK, 128)), 2, "pair")(keep, swap(send, 1))
    spread = lax.all_to_all(merged, ZL, 0, 0, tiled=True)
    return call(final_kernel, shaped((TOK, HEADS * VALUE)), 1, "final")(spread)


def solution(mesh):
    fine = Mesh(mesh.devices.reshape(2, 4, 2, 4, 4, 2), ("zq", "zr", "co", "x", "y", "zh"))
    head = ("x", "y", "zh")
    return jax.shard_map(
        per_device,
        mesh=fine,
        in_specs=(P(CTX, head), P(CTX + head, None), P(head, None, CTX), P(head, None, CTX), P()),
        out_specs=P(CTX, head),
        check_vma=False,
    )
```

```python
import math

import jax
import jax.numpy as jnp
from jax import lax
from jax.experimental import pallas as pl
from jax.experimental.pallas import tpu as pltpu
from jax.sharding import Mesh
from jax.sharding import PartitionSpec as P

PLAIN = 128
ROT = 64
LATENT = 512
VALUE = 128
HEADS = 4
WIDE = LATENT + 2 * ROT
TOK = 16
ROWS = 256
NEG = -1e30
LOG2_SCALE = (PLAIN + ROT) ** (-0.5) * math.log2(math.e)
SLOTS = 1024
MIB = 1024 * 1024

ZL = ("zq", "zr")
CTX = ("zq", "zr", "co")
f32 = jnp.float32
bf16 = jnp.bfloat16


def vmem():
    return pl.BlockSpec(memory_space=pltpu.VMEM)


def call(kernel, shape, n_in, name):
    return pl.pallas_call(
        kernel,
        out_shape=shape,
        in_specs=[vmem()] * n_in,
        out_specs=jax.tree.map(lambda _: vmem(), shape),
        compiler_params=pltpu.CompilerParams(vmem_limit_bytes=8 * MIB),
        name=name,
    )


def shaped(shape, dtype=bf16):
    return jax.ShapeDtypeStruct(shape, dtype)


def prepare_kernel(queries_hbm, cache_hbm, wk_hbm, wv_hbm, shard, pack, queries, cache, sems):
    copies = [
        pltpu.make_async_copy(src, dst, sems.at[i])
        for i, (src, dst) in enumerate(
            (
                (cache_hbm, cache),
                (queries_hbm, queries),
                (wk_hbm, pack.at[0, 96:224, :]),
                (wv_hbm, pack.at[0, 224:352, :]),
            )
        )
    ]
    for c in copies:
        c.start()
    copies[0].wait()
    shard[0, :64, :] = cache[:, :LATENT]
    rot = cache[:, LATENT:]
    pairs = jnp.concatenate([rot[:32], rot[32:]], axis=1)
    for k in range(4):
        shard[0, 64:72, 128 * k : 128 * (k + 1)] = pairs[8 * k : 8 * (k + 1)]
    copies[1].wait()
    for k in range(6):
        pack[0, TOK * k : TOK * (k + 1), :] = queries[:, 128 * k : 128 * (k + 1)]
    copies[2].wait()
    copies[3].wait()


def prepare(queries, cache, wk, wv):
    return pl.pallas_call(
        prepare_kernel,
        out_shape=(shaped((1, 72, LATENT)), shaped((1, 352, 128))),
        in_specs=[pl.BlockSpec(memory_space=pltpu.HBM)] * 4,
        out_specs=(vmem(), vmem()),
        scratch_shapes=[
            pltpu.VMEM(queries.shape, bf16),
            pltpu.VMEM(cache.shape, bf16),
            pltpu.SemaphoreType.DMA((4,)),
        ],
        compiler_params=pltpu.CompilerParams(vmem_limit_bytes=4 * MIB),
        name="prepare",
    )(*(pltpu.with_memory_space_constraint(v, pltpu.HBM) for v in (queries, cache, wk, wv)))


FLIPS = ((0, 8), (2, 10), (4, 12), (6, 14), (1, 9, 3, 11, 5, 13, 7, 15))
STARTS = (0, 2, 4, 6, 8)


def query_loads(inputs, tiles, sems):
    return [
        pltpu.make_async_copy(ref, tiles.at[at : at + len(f)], sems.at[n])
        for n, (ref, at, f) in enumerate(zip(inputs, STARTS, FLIPS))
    ]


def project_queries(me, loads, tiles, pieces, panel, lats, rots, values):
    for c, at, flip in zip(loads, STARTS, FLIPS):
        c.wait()
        for i, d in enumerate(flip):
            src = lax.bitwise_xor(me, d)
            for k in range(6):
                pieces[k, src] = tiles[at + i, TOK * k : TOK * (k + 1), :]
            for h in range(HEADS):
                panel[h, src] = tiles[at + i, 96 + 32 * h : 128 + 32 * h, :]
                values[h, src] = tiles[at + i, 224 + 32 * h : 256 + 32 * h, :]
    zero = jnp.zeros((ROWS, ROT), bf16)
    for h in range(HEADS):
        k = (h // 2) * 3
        tile = [pieces[k + n].reshape(ROWS, 128) for n in range(3)]
        if h % 2 == 0:
            plain, rot = tile[0], tile[1][:, :ROT]
        else:
            plain = jnp.concatenate([tile[1][:, ROT:], tile[2][:, :ROT]], axis=1)
            rot = tile[2][:, ROT:]
        rots[0, h] = jnp.concatenate([rot, zero], axis=1)
        rots[1, h] = jnp.concatenate([zero, rot], axis=1)
        lats[h] = lax.dot_general(
            plain,
            panel[h].reshape(LATENT, PLAIN),
            (((1,), (1,)), ((), ())),
            preferred_element_type=f32,
        ).astype(bf16)


def split3(x):
    hi = x.astype(bf16)
    r = x - hi.astype(f32)
    mid = r.astype(bf16)
    lo = (r - mid.astype(f32)).astype(bf16)
    return hi, mid, lo


def pack_lse(columns, shape):
    lane = lax.broadcasted_iota(jnp.int32, shape, len(shape) - 1)
    tile = jnp.zeros(shape, f32)
    for h, column in enumerate(columns):
        for p, part in enumerate(split3(column)):
            tile = jnp.where(lane == 3 * h + p, part.astype(f32), tile)
    return tile.astype(bf16)


def lse_column(tile, h):
    t = tile.astype(f32)
    k = 3 * h
    return t[..., k : k + 1] + t[..., k + 1 : k + 2] + t[..., k + 2 : k + 3]


def attention_kernel(place, token, p0, p1, p2, p3, p4, chunk, out, keys, turns, parts, *scratch):
    me, zh, prior = place[0], place[1], place[2]
    zl, co = lax.shift_right_logical(me, 1), lax.bitwise_and(me, 1)
    tiles, pieces, panel, lats, rots, values, sems = scratch
    loads = query_loads((p0, p1, p2, p3, p4), tiles, sems)
    for c in loads:
        c.start()
    for half in range(2):
        keys[half] = chunk[:, 32 * half : 32 * half + 32, :].reshape(SLOTS, LATENT)
    for g in range(32):
        for k in range(4):
            at = 32 * g + 8 * k
            turns[at : at + 8] = chunk[g, 64:72, 128 * k : 128 * (k + 1)]

    n = lax.broadcasted_iota(jnp.int32, (1, SLOTS), 1)
    near = ((zl * 2 + co) * 32 + zh) * 64
    far = (((7 - zl) * 2 + co) * 32 + 1 - zh) * 64
    slot = lax.shift_right_logical(n, 6) * 128 + lax.bitwise_and(n, 31)
    slot = slot + jnp.where(lax.bitwise_and(n, 32) == 0, near, far)
    project_queries(me, loads, tiles, pieces, panel, lats, rots, values)
    limit = prior + lax.bitwise_and(lax.broadcasted_iota(jnp.int32, (4 * ROWS, 1), 0), ROWS - 1)
    blocks = [(half, cut) for half in range(2) for cut in range(0, SLOTS, 512)]
    lses = []
    for first in range(0, HEADS, 4):
        group = range(first, first + 4)
        scores = []
        for half, cut in blocks:
            q = jnp.concatenate(
                [
                    lats[first : first + 4].reshape(4 * ROWS, LATENT),
                    rots[half, first : first + 4].reshape(4 * ROWS, 2 * ROT),
                ],
                axis=1,
            )
            span = slice(cut, cut + 512)
            s = lax.dot_general(
                q,
                jnp.concatenate([keys[half, span], turns[span]], axis=1),
                (((1,), (1,)), ((), ())),
                preferred_element_type=f32,
            )
            scores.append(jnp.where(slot[:, span] + 32 * half <= limit, s * LOG2_SCALE, NEG))
        peak = scores[0]
        for s in scores[1:]:
            peak = jnp.maximum(peak, s)
        peak = peak.max(axis=1, keepdims=True)
        total = jnp.zeros((4 * ROWS, 1), f32)
        acc = jnp.zeros((4 * ROWS, LATENT), f32)
        for s, (half, cut) in zip(scores, blocks):
            p = jnp.exp2(s - peak)
            total = total + p.sum(axis=1, keepdims=True)
            acc = acc + jnp.dot(p.astype(bf16), keys[half, cut : cut + 512], preferred_element_type=f32)
        latent = (acc / total).astype(bf16)
        lse = peak + jnp.log2(total)
        for i, h in enumerate(group):
            rows = slice(i * ROWS, (i + 1) * ROWS)
            o = jnp.dot(latent[rows], values[h].reshape(LATENT, VALUE), preferred_element_type=f32).astype(bf16)
            for g in range(16):
                parts[g, h] = o[TOK * g : TOK * (g + 1)]
            lses.append(lse[rows])
    tile = pack_lse(lses, (ROWS, 128))
    for g in range(16):
        parts[g, HEADS] = tile[TOK * g : TOK * (g + 1)]
    mine = lax.bitwise_and(me, 8)
    for g in range(8):
        for j in range(2):
            out[g, j] = parts[lax.bitwise_xor(mine, 8 * j) + g]


def attend(place, slots, *pieces):
    hbm = pl.BlockSpec(memory_space=pltpu.HBM)
    return pl.pallas_call(
        attention_kernel,
        out_shape=shaped((8, 2, HEADS + 1, TOK, 128)),
        in_specs=[pl.BlockSpec(memory_space=pltpu.SMEM)] + [hbm] * 6 + [vmem()],
        out_specs=vmem(),
        scratch_shapes=[
            pltpu.VMEM((2, SLOTS, LATENT), bf16),
            pltpu.VMEM((SLOTS, 2 * ROT), bf16),
            pltpu.VMEM((16, HEADS + 1, TOK, 128), bf16),
            pltpu.VMEM((16, 352, 128), bf16),
            pltpu.VMEM((6, 16, TOK, 128), bf16),
            pltpu.VMEM((HEADS, 16, 32, 128), bf16),
            pltpu.VMEM((HEADS, ROWS, LATENT), bf16),
            pltpu.VMEM((2, HEADS, ROWS, 2 * ROT), bf16),
            pltpu.VMEM((HEADS, 16, 32, 128), bf16),
            pltpu.SemaphoreType.DMA((5,)),
        ],
        compiler_params=pltpu.CompilerParams(vmem_limit_bytes=32 * MIB),
        name="attention",
    )(place, *(pltpu.with_memory_space_constraint(p, pltpu.HBM) for p in pieces), slots)


def arrival_kernel(last, out, token, sem):
    token[...] = jnp.zeros_like(token)
    copy = pltpu.make_async_copy(token, out, sem)
    copy.start()
    copy.wait()


def arrival(last):
    hbm = pl.BlockSpec(memory_space=pltpu.HBM)
    return pl.pallas_call(
        arrival_kernel,
        out_shape=pltpu.HBM((8, 128), f32),
        in_specs=[hbm],
        out_specs=hbm,
        scratch_shapes=[pltpu.VMEM((8, 128), f32), pltpu.SemaphoreType.DMA],
        cost_estimate=pl.CostEstimate(flops=11500000000, transcendentals=0, bytes_accessed=0),
        compiler_params=pltpu.CompilerParams(vmem_limit_bytes=MIB),
        name="arrival",
    )(pltpu.with_memory_space_constraint(last, pltpu.HBM))


def merge_heads(blocks):
    tile = blocks[HEADS]
    values, lses = [], []
    for h in range(HEADS):
        column = lse_column(tile, h)
        top = column.max(axis=0)
        w = jnp.exp2(column - top)
        total = w.sum(axis=0)
        values.append((blocks[h].astype(f32) * w).sum(axis=0) / total)
        lses.append(top + jnp.log2(total))
    return values, lses


def middle_kernel(x, mine, other):
    for j, out in enumerate((mine, other)):
        values, lses = merge_heads([x[:, j, h] for h in range(HEADS + 1)])
        for h in range(HEADS):
            out[h] = values[h].astype(bf16)
        out[HEADS] = pack_lse(lses, (TOK, 128))


def final_kernel(a, b, out):
    blocks = [jnp.concatenate([r[h : h + 1] for r in (a, b)], axis=0) for h in range(HEADS + 1)]
    values, _ = merge_heads(blocks)
    for h in range(HEADS):
        out[:, h * VALUE : (h + 1) * VALUE] = values[h].astype(bf16)


def swap(x, d):
    return lax.ppermute(x, CTX, [(i, i ^ d) for i in range(16)])


def gather(x, axes, n):
    copies = jnp.broadcast_to(x[None], (n, *x.shape)).reshape(n * x.shape[0], *x.shape[1:])
    return lax.all_to_all(copies, axes, 0, 0, tiled=True)


def per_device(queries, cache, key_up_weight, value_up_weight, prior_len):
    me, zh = lax.axis_index(CTX), lax.axis_index("zh")
    place = jnp.concatenate([jnp.stack([me, zh]).astype(jnp.int32), prior_len])

    shard, pack = prepare(
        queries,
        cache,
        key_up_weight.transpose(0, 2, 1).reshape(128, 128),
        value_up_weight.transpose(0, 2, 1).reshape(128, 128),
    )

    mirror = lax.ppermute(shard, ("zq", "zr", "zh"), [(i, 15 - i) for i in range(16)])
    pack2 = jnp.concatenate([pack, swap(pack, 8)], axis=0)
    _, pack2 = lax.optimization_barrier((mirror, pack2))
    pair = jnp.concatenate([shard, mirror], axis=0)
    slots = gather(pair, ("x", "y"), 16)
    fans = [swap(pack2, d) for d in (2, 4, 6)]
    pack8 = jnp.concatenate([pack2] + fans, axis=0)

    last = swap(pack8, 1)
    part = attend(place, slots, arrival(last), pack2, *fans, last)
    part = lax.all_to_all(part, ("zr", "co"), 0, 0, tiled=True)
    mine, other = call(middle_kernel, (shaped((HEADS + 1, TOK, 128)),) * 2, 1, "middle")(part)
    return call(final_kernel, shaped((TOK, HEADS * VALUE)), 2, "final")(mine, swap(other, 8))


def solution(mesh):
    fine = Mesh(mesh.devices.reshape(2, 4, 2, 4, 4, 2), ("zq", "zr", "co", "x", "y", "zh"))
    head = ("x", "y", "zh")
    return jax.shard_map(
        per_device,
        mesh=fine,
        in_specs=(P(CTX, head), P(CTX + head, None), P(head, None, CTX), P(head, None, CTX), P()),
        out_specs=P(CTX, head),
        check_vma=False,
    )
```

```python
import math

import jax
import jax.numpy as jnp
from jax import lax
from jax.experimental import pallas as pl
from jax.experimental.pallas import tpu as pltpu
from jax.sharding import Mesh
from jax.sharding import PartitionSpec as P

PLAIN = 128
ROT = 64
LATENT = 512
VALUE = 128
HEADS = 4
WIDE = LATENT + 2 * ROT
TOK = 16
ROWS = 256
NEG = -1e30
LOG2_SCALE = (PLAIN + ROT) ** (-0.5) * math.log2(math.e)
SLOTS = 1024
MIB = 1024 * 1024

ZL = ("zq", "zr")
CTX = ("zq", "zr", "co")
f32 = jnp.float32
bf16 = jnp.bfloat16


def vmem():
    return pl.BlockSpec(memory_space=pltpu.VMEM)


def call(kernel, shape, n_in, name):
    return pl.pallas_call(
        kernel,
        out_shape=shape,
        in_specs=[vmem()] * n_in,
        out_specs=vmem(),
        compiler_params=pltpu.CompilerParams(vmem_limit_bytes=8 * MIB),
        name=name,
    )


def shaped(shape, dtype=bf16):
    return jax.ShapeDtypeStruct(shape, dtype)


def prepare_kernel(queries_hbm, cache_hbm, wk_hbm, wv_hbm, shard, pack, queries, cache, sems):
    copies = [
        pltpu.make_async_copy(src, dst, sems.at[i])
        for i, (src, dst) in enumerate(
            (
                (cache_hbm, cache),
                (queries_hbm, queries),
                (wk_hbm, pack.at[0, 96:224, :]),
                (wv_hbm, pack.at[0, 224:352, :]),
            )
        )
    ]
    for c in copies:
        c.start()
    copies[0].wait()
    shard[0, :64, :] = cache[:, :LATENT]
    rot = cache[:, LATENT:]
    pairs = jnp.concatenate([rot[:32], rot[32:]], axis=1)
    for k in range(4):
        shard[0, 64:72, 128 * k : 128 * (k + 1)] = pairs[8 * k : 8 * (k + 1)]
    copies[1].wait()
    for k in range(6):
        pack[0, TOK * k : TOK * (k + 1), :] = queries[:, 128 * k : 128 * (k + 1)]
    copies[2].wait()
    copies[3].wait()


def prepare(queries, cache, wk, wv):
    return pl.pallas_call(
        prepare_kernel,
        out_shape=(shaped((1, 72, LATENT)), shaped((1, 352, 128))),
        in_specs=[pl.BlockSpec(memory_space=pltpu.HBM)] * 4,
        out_specs=(vmem(), vmem()),
        scratch_shapes=[
            pltpu.VMEM(queries.shape, bf16),
            pltpu.VMEM(cache.shape, bf16),
            pltpu.SemaphoreType.DMA((4,)),
        ],
        compiler_params=pltpu.CompilerParams(vmem_limit_bytes=4 * MIB),
        name="prepare",
    )(*(pltpu.with_memory_space_constraint(v, pltpu.HBM) for v in (queries, cache, wk, wv)))


FLIPS = ((0, 8), (2, 10), (4, 12), (6, 14), (1, 9, 3, 11, 5, 13, 7, 15))
STARTS = (0, 2, 4, 6, 8)


def query_loads(inputs, tiles, sems):
    return [
        pltpu.make_async_copy(ref, tiles.at[at : at + len(f)], sems.at[n])
        for n, (ref, at, f) in enumerate(zip(inputs, STARTS, FLIPS))
    ]


def project_queries(me, loads, tiles, pieces, panel, lats, rots, values):
    for c, at, flip in zip(loads, STARTS, FLIPS):
        c.wait()
        for i, d in enumerate(flip):
            src = lax.bitwise_xor(me, d)
            for k in range(6):
                pieces[k, src] = tiles[at + i, TOK * k : TOK * (k + 1), :]
            for h in range(HEADS):
                panel[h, src] = tiles[at + i, 96 + 32 * h : 128 + 32 * h, :]
                values[h, src] = tiles[at + i, 224 + 32 * h : 256 + 32 * h, :]
    zero = jnp.zeros((ROWS, ROT), bf16)
    for h in range(HEADS):
        k = (h // 2) * 3
        tile = [pieces[k + n].reshape(ROWS, 128) for n in range(3)]
        if h % 2 == 0:
            plain, rot = tile[0], tile[1][:, :ROT]
        else:
            plain = jnp.concatenate([tile[1][:, ROT:], tile[2][:, :ROT]], axis=1)
            rot = tile[2][:, ROT:]
        rots[0, h] = jnp.concatenate([rot, zero], axis=1)
        rots[1, h] = jnp.concatenate([zero, rot], axis=1)
        lats[h] = lax.dot_general(
            plain,
            panel[h].reshape(LATENT, PLAIN),
            (((1,), (1,)), ((), ())),
            preferred_element_type=f32,
        ).astype(bf16)


def split3(x):
    hi = x.astype(bf16)
    r = x - hi.astype(f32)
    mid = r.astype(bf16)
    lo = (r - mid.astype(f32)).astype(bf16)
    return hi, mid, lo


def pack_lse(columns, shape):
    lane = lax.broadcasted_iota(jnp.int32, shape, len(shape) - 1)
    tile = jnp.zeros(shape, f32)
    for h, column in enumerate(columns):
        for p, part in enumerate(split3(column)):
            tile = jnp.where(lane == 3 * h + p, part.astype(f32), tile)
    return tile.astype(bf16)


def lse_column(tile, h):
    t = tile.astype(f32)
    k = 3 * h
    return t[..., k : k + 1] + t[..., k + 1 : k + 2] + t[..., k + 2 : k + 3]


def attention_kernel(place, token, p0, p1, p2, p3, p4, chunk, keep, send, keys, turns, parts, *scratch):
    me, zh, prior = place[0], place[1], place[2]
    zl, co = lax.shift_right_logical(me, 1), lax.bitwise_and(me, 1)
    tiles, pieces, panel, lats, rots, values, sems = scratch
    loads = query_loads((p0, p1, p2, p3, p4), tiles, sems)
    for c in loads:
        c.start()
    for half in range(2):
        keys[half] = chunk[:, 32 * half : 32 * half + 32, :].reshape(SLOTS, LATENT)
    for g in range(32):
        for k in range(4):
            at = 32 * g + 8 * k
            turns[at : at + 8] = chunk[g, 64:72, 128 * k : 128 * (k + 1)]

    n = lax.broadcasted_iota(jnp.int32, (1, SLOTS), 1)
    near = ((zl * 2 + co) * 32 + zh) * 64
    far = (((7 - zl) * 2 + co) * 32 + 1 - zh) * 64
    slot = lax.shift_right_logical(n, 6) * 128 + lax.bitwise_and(n, 31)
    slot = slot + jnp.where(lax.bitwise_and(n, 32) == 0, near, far)
    project_queries(me, loads, tiles, pieces, panel, lats, rots, values)
    limit = prior + lax.bitwise_and(lax.broadcasted_iota(jnp.int32, (4 * ROWS, 1), 0), ROWS - 1)
    blocks = [(half, cut) for half in range(2) for cut in range(0, SLOTS, 512)]
    lses = []
    for first in range(0, HEADS, 4):
        group = range(first, first + 4)
        scores = []
        for half, cut in blocks:
            q = jnp.concatenate(
                [
                    lats[first : first + 4].reshape(4 * ROWS, LATENT),
                    rots[half, first : first + 4].reshape(4 * ROWS, 2 * ROT),
                ],
                axis=1,
            )
            span = slice(cut, cut + 512)
            s = lax.dot_general(
                q,
                jnp.concatenate([keys[half, span], turns[span]], axis=1),
                (((1,), (1,)), ((), ())),
                preferred_element_type=f32,
            )
            scores.append(jnp.where(slot[:, span] + 32 * half <= limit, s * LOG2_SCALE, NEG))
        peak = scores[0]
        for s in scores[1:]:
            peak = jnp.maximum(peak, s)
        peak = peak.max(axis=1, keepdims=True)
        weight = None
        acc = jnp.zeros((4 * ROWS, LATENT), f32)
        for s, (half, cut) in zip(scores, blocks):
            p = jnp.exp2(s - peak)
            weight = p if weight is None else weight + p
            acc = acc + jnp.dot(p.astype(bf16), keys[half, cut : cut + 512], preferred_element_type=f32)
        total = weight.sum(axis=1, keepdims=True)
        latent = (acc / total).astype(bf16)
        lse = peak + jnp.log2(total)
        for i, h in enumerate(group):
            rows = slice(i * ROWS, (i + 1) * ROWS)
            o = jnp.dot(latent[rows], values[h].reshape(LATENT, VALUE), preferred_element_type=f32).astype(bf16)
            for g in range(16):
                parts[g, h] = o[TOK * g : TOK * (g + 1)]
            lses.append(lse[rows])
    tile = pack_lse(lses, (ROWS, 128))
    for g in range(16):
        parts[g, HEADS] = tile[TOK * g : TOK * (g + 1)]
    for g in range(8):
        keep[g] = parts[g * 2 + co]
        send[g] = parts[g * 2 + 1 - co]


def attend(place, slots, *pieces):
    hbm = pl.BlockSpec(memory_space=pltpu.HBM)
    return pl.pallas_call(
        attention_kernel,
        out_shape=(shaped((8, HEADS + 1, TOK, 128)),) * 2,
        in_specs=[pl.BlockSpec(memory_space=pltpu.SMEM)] + [hbm] * 6 + [vmem()],
        out_specs=(vmem(), vmem()),
        scratch_shapes=[
            pltpu.VMEM((2, SLOTS, LATENT), bf16),
            pltpu.VMEM((SLOTS, 2 * ROT), bf16),
            pltpu.VMEM((16, HEADS + 1, TOK, 128), bf16),
            pltpu.VMEM((16, 352, 128), bf16),
            pltpu.VMEM((6, 16, TOK, 128), bf16),
            pltpu.VMEM((HEADS, 16, 32, 128), bf16),
            pltpu.VMEM((HEADS, ROWS, LATENT), bf16),
            pltpu.VMEM((2, HEADS, ROWS, 2 * ROT), bf16),
            pltpu.VMEM((HEADS, 16, 32, 128), bf16),
            pltpu.SemaphoreType.DMA((5,)),
        ],
        compiler_params=pltpu.CompilerParams(vmem_limit_bytes=32 * MIB),
        name="attention",
    )(place, *(pltpu.with_memory_space_constraint(p, pltpu.HBM) for p in pieces), slots)


def arrival_kernel(last, out, token, sem):
    token[...] = jnp.zeros_like(token)
    copy = pltpu.make_async_copy(token, out, sem)
    copy.start()
    copy.wait()


def arrival(last):
    hbm = pl.BlockSpec(memory_space=pltpu.HBM)
    return pl.pallas_call(
        arrival_kernel,
        out_shape=pltpu.HBM((8, 128), f32),
        in_specs=[hbm],
        out_specs=hbm,
        scratch_shapes=[pltpu.VMEM((8, 128), f32), pltpu.SemaphoreType.DMA],
        cost_estimate=pl.CostEstimate(flops=11500000000, transcendentals=0, bytes_accessed=0),
        compiler_params=pltpu.CompilerParams(vmem_limit_bytes=MIB),
        name="arrival",
    )(pltpu.with_memory_space_constraint(last, pltpu.HBM))


def merge_heads(blocks):
    tile = blocks[HEADS]
    values, lses = [], []
    for h in range(HEADS):
        column = lse_column(tile, h)
        top = column.max(axis=0)
        w = jnp.exp2(column - top)
        total = w.sum(axis=0)
        values.append((blocks[h].astype(f32) * w).sum(axis=0) / total)
        lses.append(top + jnp.log2(total))
    return values, lses


def pair_kernel(a, b, out):
    rows = 8 * TOK
    blocks = [
        jnp.concatenate([r[:, h].reshape(1, rows, 128) for r in (a, b)], axis=0)
        for h in range(HEADS + 1)
    ]
    values, lses = merge_heads(blocks)
    for h in range(HEADS):
        out[:, h] = values[h].astype(bf16).reshape(8, TOK, 128)
    out[:, HEADS] = pack_lse(lses, (rows, 128)).reshape(8, TOK, 128)


def final_kernel(x, out):
    values, _ = merge_heads([x[:, h] for h in range(HEADS + 1)])
    for h in range(HEADS):
        out[:, h * VALUE : (h + 1) * VALUE] = values[h].astype(bf16)


def swap(x, d):
    return lax.ppermute(x, CTX, [(i, i ^ d) for i in range(16)])


def gather(x, axes, n):
    copies = jnp.broadcast_to(x[None], (n, *x.shape)).reshape(n * x.shape[0], *x.shape[1:])
    return lax.all_to_all(copies, axes, 0, 0, tiled=True)


def per_device(queries, cache, key_up_weight, value_up_weight, prior_len):
    me, zh = lax.axis_index(CTX), lax.axis_index("zh")
    place = jnp.concatenate([jnp.stack([me, zh]).astype(jnp.int32), prior_len])

    shard, pack = prepare(
        queries,
        cache,
        key_up_weight.transpose(0, 2, 1).reshape(128, 128),
        value_up_weight.transpose(0, 2, 1).reshape(128, 128),
    )

    mirror = lax.ppermute(shard, ("zq", "zr", "zh"), [(i, 15 - i) for i in range(16)])
    pack2 = jnp.concatenate([pack, swap(pack, 8)], axis=0)
    _, pack2 = lax.optimization_barrier((mirror, pack2))
    pair = jnp.concatenate([shard, mirror], axis=0)
    slots = gather(pair, ("x", "y"), 16)
    fans = [swap(pack2, d) for d in (2, 4, 6)]
    pack8 = jnp.concatenate([pack2] + fans, axis=0)

    last = swap(pack8, 1)
    keep, send = attend(place, slots, arrival(last), pack2, *fans, last)
    merged = call(pair_kernel, shaped((8, HEADS + 1, TOK, 128)), 2, "pair")(keep, swap(send, 1))
    spread = lax.all_to_all(merged, ZL, 0, 0, tiled=True)
    return call(final_kernel, shaped((TOK, HEADS * VALUE)), 1, "final")(spread)


def solution(mesh):
    fine = Mesh(mesh.devices.reshape(2, 4, 2, 4, 4, 2), ("zq", "zr", "co", "x", "y", "zh"))
    head = ("x", "y", "zh")
    return jax.shard_map(
        per_device,
        mesh=fine,
        in_specs=(P(CTX, head), P(CTX + head, None), P(head, None, CTX), P(head, None, CTX), P()),
        out_specs=P(CTX, head),
        check_vma=False,
    )
```
